32 devices in a mesh: groups: 2 (over x), att: 2 (over y), exp: 8 (over z, core).
Axes of the slice: x: 2, y: 2, z: 4, core: 2. Of those that a mesh axis runs over, the one named last changes fastest.
Arguments:
- queries: bfloat16 [1024, 4096], P(('groups', 'exp')), parts along dimension 0, may hold values from -12 to 12
- row_key_value: bfloat16 [1024, 1024], P(('groups', 'exp')), parts along dimension 0, may hold values from -12 to 12
- shared_context_cache: bfloat16 [4, 1024, 1024], P('groups', 'att'), parts along dimension 0, may hold values from -6 to 6
- branch: int32 [1024], P(('groups', 'exp')), parts along dimension 0, may hold values from 0 to 1
- sink_logits: float32 [64], replicated, may hold values from 8 to 13
- w_out: bfloat16 [4096, 2880], P(None, 'att'), may hold values from -0.09375 to 0.09375
- residual: bfloat16 [1024, 2880], P(('groups', 'exp'), 'att'), parts along dimension 0, may hold values from -20 to 20
- norm_gain: bfloat16 [2880], P('att'), may hold values from 0.099609375 to 1.8984375
- expert_ids: int32 [1024, 4], P(('groups', 'exp')), parts along dimension 0, may hold values from 0 to 7, all different within a row; in each aligned block of 64 rows (0 to 63, 64 to 127, ...) at most 64 rows name the same one
- weight_codes: int32 [1024, 4], P(('groups', 'exp')), parts along dimension 0, may hold values from 1 to 255
- w_gate: bfloat16 [8, 2880, 2880], P('exp', None, 'att'), may hold values from -0.4375 to 0.4375
- w_up: bfloat16 [8, 2880, 2880], P('exp', None, 'att'), may hold values from -0.4375 to 0.4375
- w_down: bfloat16 [8, 2880, 2880], P('exp', 'att'), may hold values from -0.013671875 to 0.013671875
Outputs:
- attended: bfloat16 [1024, 2880], P(('groups', 'exp'), 'att'), parts along dimension 0
- expert_mix: bfloat16 [1024, 2880], P(('groups', 'exp'), 'att'), parts along dimension 0
The draws below stay inside these ranges and needn't reach their ends.
There are 2 independent parts, one for each index of `groups`. The reference program is written for one: setup_inputs(seed, part) draws one part's arguments, and reference() takes and returns one part's arrays. A program takes and returns all parts, laid end to end along the dimension named above; an argument that names none is the same for every part. Nothing has to cross between parts.
Inputs may be any that keep to these rules, and one draw needn't show every extreme that they name: `expert_ids`: each row names 4 different experts; within the rows of one index of exp (aligned blocks of 64 rows) no expert is named more than 64 times, and in some block some expert is named exactly 64 times.
All inputs are finite; a program needn't handle non-finite values.
Results may differ from the reference program's by a relative error of at most 0.022.
Values may be sent and summed in bfloat16 or wider, within the bound.
A program may use at most 128 MiB of HBM per device.

```python
import math
from functools import partial
import jax
import jax.numpy as jnp
import numpy as np
from jax import lax

D = 2880
QUERY_HEADS = 64
KEY_VALUE_HEADS = 8
HEAD_SIZE = 64
FF = 2880
TOP = 4
SHARED_CONTEXTS = 2
ROWS_DEV = 64
EXPERTS = 8
DECODE_ROWS = 512
CONTEXT_TOKENS = 1024
CAP = 64
N_EXP = 8


def draw_queries(key, part):
    random_seed_key = jax.random.fold_in(key, 11)
    value_rows = jnp.clip(2.5 * jax.random.normal(random_seed_key, (DECODE_ROWS, QUERY_HEADS, HEAD_SIZE), jnp.float32), -12.0, 12.0)
    return value_rows.reshape(DECODE_ROWS, QUERY_HEADS * HEAD_SIZE).astype(jnp.bfloat16)


def draw_shared_context_cache(key, part):
    random_seed_key = jax.random.fold_in(key, 12)
    value_rows = jnp.clip(jax.random.normal(random_seed_key, (SHARED_CONTEXTS, CONTEXT_TOKENS, 2, KEY_VALUE_HEADS, HEAD_SIZE), jnp.float32), -6.0, 6.0)
    return value_rows.reshape(SHARED_CONTEXTS, CONTEXT_TOKENS, 2 * KEY_VALUE_HEADS * HEAD_SIZE).astype(jnp.bfloat16)


def draw_residual(key, part):
    column = jnp.arange(D, dtype=jnp.float32) / (D - 1)
    random_seed_key = jax.random.fold_in(key, 13)
    value_rows = jnp.clip(jax.random.normal(random_seed_key, (DECODE_ROWS, D), jnp.float32), -6.0, 6.0) * 0.4 * jnp.exp(column * math.log(3.0))[None, :]
    return value_rows.astype(jnp.bfloat16)


def plant(result, own_key, least, largest):
    shape = result.shape
    place = [jax.random.randint(jax.random.fold_in(own_key, axis), (), 0, shape[axis]) for axis in range(len(shape))]
    result = result.at[tuple(place)].set(least)
    longest = shape.index(max(shape))
    place[longest] = (place[longest] + 1) % shape[longest]
    return result.at[tuple(place)].set(largest)


def steps_of(key, extent, cuts, low, high):
    factor_of, own = 1.0, jax.random.fold_in(key, 6)
    for axis_at, parts in cuts:
        steps = jnp.exp(jax.random.uniform(jax.random.fold_in(own, axis_at), (parts,), jnp.float32, low / len(cuts), high / len(cuts)))
        factor_of = factor_of * jnp.repeat(steps, extent[axis_at] // parts).reshape([-1 if axis == axis_at else 1 for axis in range(len(extent))])
    return factor_of


def deal_out(own_key, own, number, rows, amount, top, most, skew):
    order = jax.random.permutation(own_key, amount)
    crowded, usual = load_shares(amount, rows * top, most, skew, True), load_shares(amount, rows * top, most, skew, False)
    places = jnp.arange(amount)

    def named(sizes, turn):
        used = int((sizes > 0).sum())
        fixed = max(1, used // 4)
        passed = fixed + (places - fixed + turn * (used - fixed)) % max(1, amount - fixed)
        return jnp.zeros((amount,), jnp.int32).at[order[jnp.where(places < fixed, places, passed)]].set(jnp.asarray(sizes, jnp.int32))

    sizes = jnp.where(number % 4 == 0, named(crowded, number // 4), named(usual, number - number // 4 - 1))
    mixed = jax.random.permutation(jax.random.fold_in(own, 3), amount)
    donor, taker = mixed[0:amount // 2 * 2:2], mixed[1:amount // 2 * 2:2]
    slack = jnp.minimum(sizes[donor] - 1, most - sizes[taker]) // 2
    slack = jnp.where((donor == order[0]) | (taker == order[0]) | (sizes[taker] == 0), 0, jnp.maximum(slack, 0))
    passed = jax.random.randint(jax.random.fold_in(own, 4), (amount // 2,), 0, 1 << 20) % (slack + 1)
    sizes = sizes.at[donor].add(-passed).at[taker].add(passed)
    labels = jnp.searchsorted(jnp.cumsum(sizes), jnp.arange(rows * top), side="right").astype(jnp.int32)
    listing = labels.reshape(top, rows).T
    listing = listing[jax.random.permutation(jax.random.fold_in(own, 1), rows)]
    turn = jax.random.randint(jax.random.fold_in(own, 2), (rows, 1), 0, top)
    return jnp.take_along_axis(listing, (jnp.arange(top)[None, :] + turn) % top, axis=1)


def load_shares(amount, total, most, skew, full):
    portions = [(1 << 20) // math.isqrt(grade ** skew) + 1 for grade in range(1, amount + 1)]
    largest = most if full else min(most, max(-(-total // amount), total * portions[0] // sum(portions)))
    least = 1 if total - largest >= amount - 1 else 0
    given, rest = [largest] + [least] * (amount - 1), total - largest - least * (amount - 1)
    while rest > 0:
        free = [i for i in range(1, amount) if given[i] < largest] or [i for i in range(1, amount) if given[i] < most]
        mass, left = sum([portions[i] for i in free]), rest
        for i in free:
            extra = min(most - given[i], max(1, left * portions[i] // mass), rest)
            given[i] = given[i] + extra
            rest = rest - extra
    return np.array(given)


def centred(rng, extent, width, bound, cuts=(), kind=jnp.bfloat16):
    loudness = steps_of(rng, extent, cuts, -0.22, 0.18) if cuts else 1.0
    result = jax.random.normal(rng, extent, jnp.float32) * width * loudness
    return jnp.minimum(jnp.maximum(result, -bound), bound).astype(kind)


def setup_inputs(seed: int = 0, part: int = 0) -> dict:
    keys = jax.random.split(jax.random.key(seed), 14)
    part_splits = jax.random.split(jax.random.fold_in(keys[13], part), 14)
    queries = draw_queries(jax.random.fold_in(jax.random.fold_in(keys[13], part), 71), part)
    row_key_value = centred(part_splits[1], (DECODE_ROWS, 2 * KEY_VALUE_HEADS * HEAD_SIZE), 2.0, 12.0, ((0, 8),))
    shared_context_cache = draw_shared_context_cache(jax.random.fold_in(jax.random.fold_in(keys[13], part), 71), part)
    branch = plant(jax.random.randint(part_splits[3], (DECODE_ROWS,), 0, SHARED_CONTEXTS), jax.random.fold_in(part_splits[3], 1), 0, SHARED_CONTEXTS - 1).astype(jnp.int32)
    sink_logits = jnp.clip(jax.random.uniform(keys[4], (QUERY_HEADS,), jnp.float32, 8.0, 13.0), 8.0, 13.0)
    w_out = centred(keys[5], (QUERY_HEADS * HEAD_SIZE, D), (QUERY_HEADS * HEAD_SIZE) ** -0.5, 0.09375, ((1, 2),))
    residual = draw_residual(jax.random.fold_in(jax.random.fold_in(keys[13], part), 71), part)
    norm_gain = jnp.clip(1.0 + 0.18 * jax.random.normal(keys[7], (D,), jnp.float32), 0.099609375, 1.8984375).astype(jnp.bfloat16)
    expert_ids_keys = jax.random.split(jax.random.fold_in(part_splits[8], 1), DECODE_ROWS // ROWS_DEV)
    expert_ids_turns = jax.random.permutation(jax.random.fold_in(part_splits[8], 3), DECODE_ROWS // ROWS_DEV)
    expert_ids = jax.vmap(lambda own, number: deal_out(jax.random.fold_in(part_splits[8], 2), own, number, ROWS_DEV, EXPERTS, TOP, CAP, 2))(expert_ids_keys, expert_ids_turns).reshape((DECODE_ROWS, TOP))
    weight_codes = plant(jax.random.randint(part_splits[9], (DECODE_ROWS, TOP), 1, 256), jax.random.fold_in(part_splits[9], 1), 1, 255).astype(jnp.int32)
    w_gate = centred(keys[10], (EXPERTS, D, FF), (D // 16) ** -0.5, 0.4375, ((0, 8), (2, 2)))
    w_up = centred(keys[11], (EXPERTS, D, FF), (D // 16) ** -0.5, 0.4375, ((0, 8), (2, 2)))
    w_down = centred(keys[12], (EXPERTS, FF, D), (64 * FF) ** -0.5, 0.013671875, ((0, 8), (1, 2)))
    return {"queries": queries, "row_key_value": row_key_value, "shared_context_cache": shared_context_cache, "branch": branch, "sink_logits": sink_logits, "w_out": w_out, "residual": residual, "norm_gain": norm_gain, "expert_ids": expert_ids, "weight_codes": weight_codes, "w_gate": w_gate, "w_up": w_up, "w_down": w_down}


clamp_limit = 7.0

def attend_block(packed, shared_context_cache, sink_logits):
    query_block, fresh_block, block_branch = packed
    decode_row_count = query_block.shape[0]
    heads_per_group = QUERY_HEADS // KEY_VALUE_HEADS
    score_scale = HEAD_SIZE ** (-0.5)
    grouped_heads = query_block.reshape(decode_row_count, KEY_VALUE_HEADS, heads_per_group, HEAD_SIZE).astype(jnp.float32)
    current = None
    for context_slot in range(SHARED_CONTEXTS):
        cached_key_block = shared_context_cache[context_slot, :, :KEY_VALUE_HEADS * HEAD_SIZE].reshape(-1, KEY_VALUE_HEADS, HEAD_SIZE).astype(jnp.float32)
        cached_value_block = shared_context_cache[context_slot, :, KEY_VALUE_HEADS * HEAD_SIZE:].reshape(-1, KEY_VALUE_HEADS, HEAD_SIZE).astype(jnp.float32)
        scores = jnp.einsum('rgqd,tgd->rgqt', grouped_heads, cached_key_block) * score_scale
        local_max = lax.optimization_barrier(jnp.max(scores, axis=-1))
        weights = jnp.exp(scores - local_max[..., None])
        local_total = lax.optimization_barrier(jnp.sum(weights, axis=-1))
        rounded = lax.optimization_barrier(weights.astype(jnp.bfloat16)).astype(jnp.float32)
        local_out = jnp.einsum('rgqt,tgd->rgqd', rounded, cached_value_block)
        if current is None:
            current = (local_max, local_total, local_out)
        else:
            chosen = block_branch == context_slot
            current = (jnp.where(chosen[:, None, None], local_max, current[0]), jnp.where(chosen[:, None, None], local_total, current[1]), jnp.where(chosen[:, None, None, None], local_out, current[2]))
    cache_max = current[0].reshape(decode_row_count, QUERY_HEADS)
    cache_total = current[1].reshape(decode_row_count, QUERY_HEADS)
    cache_out = current[2].reshape(decode_row_count, QUERY_HEADS, HEAD_SIZE)
    row_own_keys = fresh_block[:, :KEY_VALUE_HEADS * HEAD_SIZE].reshape(decode_row_count, KEY_VALUE_HEADS, 1, HEAD_SIZE).astype(jnp.float32)
    row_own_values = fresh_block[:, KEY_VALUE_HEADS * HEAD_SIZE:].reshape(decode_row_count, KEY_VALUE_HEADS, 1, HEAD_SIZE).astype(jnp.float32)
    own_score = (lax.optimization_barrier(jnp.sum(grouped_heads * row_own_keys, axis=-1)) * score_scale).reshape(decode_row_count, QUERY_HEADS)
    row_own_values = jnp.broadcast_to(row_own_values, (decode_row_count, KEY_VALUE_HEADS, heads_per_group, HEAD_SIZE)).reshape(decode_row_count, QUERY_HEADS, HEAD_SIZE)
    sink_row = sink_logits.astype(jnp.float32)[None, :]
    peak = jnp.maximum(jnp.maximum(cache_max, own_score), sink_row)
    cache_factor = jnp.exp(cache_max - peak)
    own_factor = jnp.exp(own_score - peak)
    sink_factor = jnp.exp(sink_row - peak)
    denominator = cache_total * cache_factor + own_factor + sink_factor
    numerator = cache_out * cache_factor[..., None] + own_factor[..., None] * row_own_values
    return (numerator / denominator[..., None]).reshape(decode_row_count, QUERY_HEADS * HEAD_SIZE).astype(jnp.bfloat16)

def reference(queries, row_key_value, shared_context_cache, branch, sink_logits, w_out, residual, norm_gain, expert_ids, weight_codes, w_gate, w_up, w_down):
    total_rows = queries.shape[0]
    blocks = total_rows // ROWS_DEV
    packed = (queries.reshape(blocks, ROWS_DEV, -1), row_key_value.reshape(blocks, ROWS_DEV, -1), branch.reshape(blocks, ROWS_DEV))
    attention = lax.map(partial(attend_block, shared_context_cache=shared_context_cache, sink_logits=sink_logits), packed)
    attention = attention.reshape(total_rows, QUERY_HEADS * HEAD_SIZE)
    hidden = residual.astype(jnp.float32) + jnp.dot(attention, w_out, preferred_element_type=jnp.float32)
    attended = hidden.astype(jnp.bfloat16)
    squares = lax.optimization_barrier(jnp.sum(hidden * hidden, axis=1))
    inverse = lax.rsqrt(squares / D + 1e-05)
    normed = (hidden * inverse[:, None] * norm_gain.astype(jnp.float32)[None, :]).astype(jnp.bfloat16)
    shares = weight_codes.astype(jnp.float32)
    shares = shares / lax.optimization_barrier(jnp.sum(shares, axis=1, keepdims=True))
    room = N_EXP * CAP

    def one_expert(mixture, packed_expert):
        expert, gate_weight, up_weight, down_weight = packed_expert
        expert_hit = expert_ids == expert
        routed = jnp.any(expert_hit, axis=1)
        share = lax.optimization_barrier(jnp.sum(jnp.where(expert_hit, shares, jnp.zeros_like(shares)), axis=1))
        chosen = jnp.nonzero(routed, size=room, fill_value=0)[0].astype(jnp.int32)
        valid = (jnp.arange(room, dtype=jnp.int32) < jnp.sum(routed.astype(jnp.int32))).astype(jnp.float32)
        rows_in = normed[chosen]
        gate_sum = jnp.minimum(jnp.dot(rows_in, gate_weight, preferred_element_type=jnp.float32), clamp_limit)
        up_sum = jnp.clip(jnp.dot(rows_in, up_weight, preferred_element_type=jnp.float32), -clamp_limit, clamp_limit)
        active = (gate_sum * jax.nn.sigmoid(1.702 * gate_sum) * (up_sum + 1.0)).astype(jnp.bfloat16)
        output = jnp.dot(active, down_weight, preferred_element_type=jnp.float32).astype(jnp.bfloat16)
        contribution = output.astype(jnp.float32) * (share[chosen] * valid)[:, None]
        return (mixture.at[chosen].add(contribution), None)
    start_mix = jnp.zeros((total_rows, D), jnp.float32)
    mixture, ignored = lax.scan(one_expert, start_mix, (jnp.arange(EXPERTS, dtype=jnp.int32), w_gate, w_up, w_down))
    return (attended, mixture.astype(jnp.bfloat16))
```

```python
import functools

import jax
import jax.numpy as jnp
from jax import lax
from jax.experimental import pallas as pl
from jax.experimental.pallas import tpu as pltpu
from jax.sharding import PartitionSpec as P

D = 2880
QUERY_HEADS = 64
KEY_VALUE_HEADS = 8
HEAD_SIZE = 64
TOP = 4
SHARED_CONTEXTS = 2


MESH = pl.DeviceIdType.MESH
clamp_limit = 7.0


def combined_all(x, axis, combine):
    everything = jax.tree.map(
        lambda part, kind: lax.all_gather(part.astype(kind), axis),
        x,
        jax.tree.map(lambda a: jnp.bfloat16 if a.dtype == jnp.float32 else a.dtype, x),
    )

    def take(k):
        return jax.tree.map(lambda part, own: part[k].astype(own.dtype), everything, x)

    return lax.fori_loop(
        1, lax.axis_size(axis), lambda k, so_far: combine(so_far, take(k)), take(0)
    )


def merge_parts(first, second):
    first_max, first_total, first_out = first
    second_max, second_total, second_out = second
    joint_max = jnp.maximum(first_max, second_max)
    first_factor = jnp.exp(first_max - joint_max)
    second_factor = jnp.exp(second_max - joint_max)
    joint_total = first_total * first_factor + second_total * second_factor
    decode_row_count, head_count = first_max.shape
    joint_out = (
        first_out.reshape(decode_row_count, head_count, -1) * first_factor[:, :, None]
        + second_out.reshape(decode_row_count, head_count, -1) * second_factor[:, :, None]
    )
    return (joint_max, joint_total, joint_out.reshape(decode_row_count, -1))


def local_partials(grouped_heads, shared_context_cache, branch):
    decode_row_count = grouped_heads.shape[0]
    score_scale = HEAD_SIZE ** (-0.5)
    current = None
    for context_slot in range(SHARED_CONTEXTS):
        cached_key_block = shared_context_cache[
            context_slot, :, : KEY_VALUE_HEADS * HEAD_SIZE
        ].reshape(-1, KEY_VALUE_HEADS, HEAD_SIZE)
        cached_value_block = shared_context_cache[
            context_slot, :, KEY_VALUE_HEADS * HEAD_SIZE :
        ].reshape(-1, KEY_VALUE_HEADS, HEAD_SIZE)
        scores = (
            jnp.einsum(
                "rgqd,tgd->rgqt",
                grouped_heads,
                cached_key_block,
                preferred_element_type=jnp.float32,
            )
            * score_scale
        )
        local_max = jnp.max(scores, axis=-1)
        weights = jnp.exp(scores - local_max[..., None])
        local_total = jnp.sum(weights, axis=-1)
        local_out = jnp.einsum(
            "rgqt,tgd->rgqd",
            weights.astype(jnp.bfloat16),
            cached_value_block,
            preferred_element_type=jnp.float32,
        )
        if current is None:
            current = (local_max, local_total, local_out)
        else:
            chosen = branch == context_slot
            current = (
                jnp.where(chosen[:, None, None], local_max, current[0]),
                jnp.where(chosen[:, None, None], local_total, current[1]),
                jnp.where(chosen[:, None, None, None], local_out, current[2]),
            )
    return (
        current[0].reshape(decode_row_count, QUERY_HEADS),
        current[1].reshape(decode_row_count, QUERY_HEADS),
        current[2].reshape(decode_row_count, QUERY_HEADS * HEAD_SIZE),
    )


def finish_attention(merged, grouped_heads, row_key_value, sink_logits):
    decode_row_count = grouped_heads.shape[0]
    heads_per_group = QUERY_HEADS // KEY_VALUE_HEADS
    score_scale = HEAD_SIZE ** (-0.5)
    cache_max, cache_total, cache_out = merged
    row_own_keys = (
        row_key_value[:, : KEY_VALUE_HEADS * HEAD_SIZE]
        .reshape(decode_row_count, KEY_VALUE_HEADS, 1, HEAD_SIZE)
        .astype(jnp.float32)
    )
    row_own_values = (
        row_key_value[:, KEY_VALUE_HEADS * HEAD_SIZE :]
        .reshape(decode_row_count, KEY_VALUE_HEADS, 1, HEAD_SIZE)
        .astype(jnp.float32)
    )
    own_score = (
        jnp.sum(grouped_heads.astype(jnp.float32) * row_own_keys, axis=-1) * score_scale
    ).reshape(decode_row_count, QUERY_HEADS)
    row_own_values = jnp.broadcast_to(
        row_own_values, (decode_row_count, KEY_VALUE_HEADS, heads_per_group, HEAD_SIZE)
    ).reshape(decode_row_count, QUERY_HEADS, HEAD_SIZE)
    sink_row = sink_logits[None, :]
    peak = jnp.maximum(jnp.maximum(cache_max, own_score), sink_row)
    cache_factor = jnp.exp(cache_max - peak)
    own_factor = jnp.exp(own_score - peak)
    sink_factor = jnp.exp(sink_row - peak)
    denominator = cache_total * cache_factor + own_factor + sink_factor
    numerator = (
        cache_out.reshape(decode_row_count, QUERY_HEADS, HEAD_SIZE) * cache_factor[..., None]
        + own_factor[..., None] * row_own_values
    )
    return (
        (numerator / denominator[..., None])
        .reshape(decode_row_count, QUERY_HEADS * HEAD_SIZE)
        .astype(jnp.bfloat16)
    )

def moe_kernel(
    n,
    u_ref,
    meta_ref,
    wg_hbm,
    wu_hbm,
    wd_hbm,
    out_ref,
    wg,
    wu,
    wd,
    X,
    META,
    act_ref,
    P_ref,
    CS,
    SR,
    SL,
    RR,
    RL,
    YS,
    YR,
    wsem,
    xsend,
    xrecv,
    msend,
    mrecv,
    csend,
    crecv,
    rsend,
    rrecv,
    ysend,
    yrecv,
):
    rings = n // 2
    half_ring = rings // 2
    rows = u_ref.shape[0]
    width = u_ref.shape[1]
    half_rows = rows // 2
    experts = meta_ref.shape[0]
    a = lax.axis_index("att")
    e = lax.axis_index("exp")
    z = e // 2
    c = e % 2

    def at(offset):
        return lax.rem(z + offset + rings, rings)

    def lane(offset):
        return at(offset) * 2 + c

    right = {"exp": lane(1)}
    left = {"exp": lane(-1)}
    mate = {"exp": z * 2 + 1 - c}
    across = {"att": 1 - a}

    loads = [
        pltpu.make_async_copy(wg_hbm.at[0], wg, wsem.at[0]),
        pltpu.make_async_copy(wu_hbm.at[0], wu, wsem.at[1]),
        pltpu.make_async_copy(wd_hbm.at[0], wd, wsem.at[2]),
    ]
    for load in loads:
        load.start()

    barrier = pltpu.get_barrier_semaphore()
    for target in (right, left, mate, across):
        pl.semaphore_signal(barrier, inc=1, device_id=target, device_id_type=MESH)
    pl.semaphore_wait(barrier, 4)

    pending = []
    counter = [0]

    def send(src_x, src_m, h, idx, target, part=None):
        k = counter[0]
        counter[0] += 1
        if part is None:
            dst_x, slot = X.at[h, idx], 0
        else:
            dst_x, slot = X.at[h, idx, pl.ds(part * half_rows, half_rows)], part
        x_copy = pltpu.make_async_remote_copy(
            src_ref=src_x,
            dst_ref=dst_x,
            send_sem=xsend.at[k],
            recv_sem=xrecv.at[h, idx, slot],
            device_id=target,
            device_id_type=MESH,
        )
        x_copy.start()
        pending.append(x_copy)
        if part is None or part == 0:
            m_copy = pltpu.make_async_remote_copy(
                src_ref=src_m,
                dst_ref=META.at[h, idx],
                send_sem=msend.at[k],
                recv_sem=mrecv.at[h, idx],
                device_id=target,
                device_id_type=MESH,
            )
            m_copy.start()
            pending.append(m_copy)

    def arrived(h, idx, part=None):
        if part is None:
            ref, slot = X.at[h, idx], 0
        else:
            ref, slot = X.at[h, idx, pl.ds(part * half_rows, half_rows)], part
        pltpu.make_async_remote_copy(
            src_ref=ref,
            dst_ref=ref,
            send_sem=xsend.at[0],
            recv_sem=xrecv.at[h, idx, slot],
            device_id=mate,
            device_id_type=MESH,
        ).wait_recv()
        if part is None or part == 0:
            pltpu.make_async_remote_copy(
                src_ref=META.at[h, idx],
                dst_ref=META.at[h, idx],
                send_sem=msend.at[0],
                recv_sem=mrecv.at[h, idx],
                device_id=mate,
                device_id_type=MESH,
            ).wait_recv()

    halves = (a, 1 - a)
    send(u_ref, meta_ref, a, e, across)
    send(u_ref, meta_ref, a, e, right)
    send(u_ref, meta_ref, a, e, left)
    send(u_ref, meta_ref, a, e, mate)
    X[a, e] = u_ref[...]
    META[a, e] = meta_ref[...]
    arrived(1 - a, e)
    own = (1 - a, e)
    for target in (right, left, mate):
        send(X.at[own], META.at[own], 1 - a, e, target)

    def forward(step, h):
        from_left, from_right = lane(-step), lane(step)
        if step < half_ring:
            last = step + 1 == half_ring
            arrived(h, from_left)
            if last:
                lo = pl.ds(0, half_rows)
                send(X.at[h, from_left, lo], META.at[h, from_left], h, from_left, right, 0)
            else:
                send(X.at[h, from_left], META.at[h, from_left], h, from_left, right)
            arrived(h, from_right)
            if last:
                hi = pl.ds(half_rows, half_rows)
                send(X.at[h, from_right, hi], None, h, from_right, left, 1)
            else:
                send(X.at[h, from_right], META.at[h, from_right], h, from_right, left)
            send(X.at[h, from_left], META.at[h, from_left], h, from_left, mate)
            send(X.at[h, from_right], META.at[h, from_right], h, from_right, mate)
        else:
            arrived(h, from_left, 0)
            arrived(h, from_left, 1)
            send(X.at[h, from_left], META.at[h, from_left], h, from_left, mate)

    def mates(step, h):
        arrived(h, at(-step) * 2 + 1 - c)
        if 0 < step < half_ring:
            arrived(h, at(step) * 2 + 1 - c)

    eye = lax.broadcasted_iota(jnp.int32, (rows, rows), 0) == lax.broadcasted_iota(
        jnp.int32, (rows, rows), 1
    )

    def upright(row):
        return jnp.sum(jnp.where(eye, jnp.broadcast_to(row, (rows, rows)), 0.0), axis=1, keepdims=True)

    def run_chunk(offsets):
        blocks = [at(o) * 2 + k for o in offsets for k in range(2)]
        count = len(blocks) * rows
        x0 = jnp.concatenate([X[0, b] for b in blocks], axis=0)
        x1 = jnp.concatenate([X[1, b] for b in blocks], axis=0)
        shares, inverses = [], []
        pick = lax.broadcasted_iota(jnp.int32, (experts, 2 * rows), 0) == e
        for b in blocks:
            squares = META[0, b][0:1, rows : 2 * rows] + META[1, b][0:1, rows : 2 * rows]
            inverses.append(upright(lax.rsqrt(squares / (2 * width) + 1e-05)))
            mine = jnp.sum(jnp.where(pick, META[0, b], 0.0), axis=0, keepdims=True)
            shares.append(upright(mine[:, :rows]))
        inverse = jnp.concatenate(inverses, axis=0)
        share = jnp.concatenate(shares, axis=0)

        def first(start, size):
            cols = pl.ds(start, size)
            g = jnp.dot(x0, wg[:width, cols], preferred_element_type=jnp.float32)
            g += jnp.dot(x1, wg[width:, cols], preferred_element_type=jnp.float32)
            u = jnp.dot(x0, wu[:width, cols], preferred_element_type=jnp.float32)
            u += jnp.dot(x1, wu[width:, cols], preferred_element_type=jnp.float32)
            g = jnp.minimum(g * inverse, clamp_limit)
            u = jnp.clip(u * inverse, -clamp_limit, clamp_limit)
            act_ref[:, cols] = (g * jax.nn.sigmoid(1.702 * g) * (u + 1.0)).astype(jnp.bfloat16)

        def second(start, size):
            cols = pl.ds(start, size)
            y = jnp.dot(act_ref[...], wd[:, cols], preferred_element_type=jnp.float32)
            y = (y * share).astype(jnp.bfloat16)
            for k, b in enumerate(blocks):
                P_ref[b, :, cols] = y[k * rows : (k + 1) * rows]

        def tiled(body, total, tile):
            whole_tiles = total // tile

            @pl.loop(0, whole_tiles)
            def _(i):
                body(pl.multiple_of(i * tile, tile), tile)

            if total % tile:
                body(whole_tiles * tile, total % tile)

        return tiled, first, second

    order = [0]
    for s in range(1, half_ring):
        order += [-s, s]
    order += [half_ring]
    chunks = [order[k : k + 2] for k in range(0, len(order), 2)]

    c_copies = []

    def swap(offset):
        dest = at(offset)
        k = offset % rings
        copy = pltpu.make_async_remote_copy(
            src_ref=P_ref.at[dest * 2 + 1 - c],
            dst_ref=CS.at[dest],
            send_sem=csend.at[k],
            recv_sem=crecv.at[dest],
            device_id=mate,
            device_id_type=MESH,
        )
        copy.start()
        return copy

    for step in range(1, half_ring + 1):
        for h in halves:
            forward(step, h)
    for step in range(0, half_ring + 1):
        for h in halves:
            mates(step, h)
    loads[0].wait()
    loads[1].wait()
    loads[2].wait()
    swaps = {}
    for offsets in chunks[::-1]:
        tiled, first, second = run_chunk(offsets)
        tiled(first, width, 256)
        tiled(second, 2 * width, 256)
        for o in offsets:
            swaps[o % rings] = swap(o)

    def chip_sum(offset):
        dest = at(offset)
        return P_ref[dest * 2 + c].astype(jnp.float32) + CS[dest].astype(jnp.float32)

    ring_copies = []

    def ring_copy(src, dst, k, d, target):
        copy = pltpu.make_async_remote_copy(
            src_ref=src,
            dst_ref=dst,
            send_sem=rsend.at[k, d - 1],
            recv_sem=rrecv.at[k, d - 1],
            device_id=target,
            device_id_type=MESH,
        )
        copy.start()
        ring_copies.append(copy)
        return copy

    coming = {}
    lo = pl.ds(0, half_rows)
    hi = pl.ds(half_rows, half_rows)
    swapped = set()

    def swap_done(offset):
        k = offset % rings
        if k not in swapped:
            swapped.add(k)
            swaps[k].wait()

    for d in range(half_ring, 0, -1):
        swap_done(d)
        swap_done(-d)
        if d == half_ring:
            total = chip_sum(d).astype(jnp.bfloat16)
            SR[d - 1, lo] = total[:half_rows]
            SL[d - 1, hi] = total[half_rows:]
            coming[0] = ring_copy(SR.at[d - 1, lo], RR.at[d - 1, lo], 0, d, right)
            coming[1] = ring_copy(SL.at[d - 1, hi], RL.at[d - 1, hi], 1, d, left)
            continue
        if d + 1 == half_ring:
            to_right = chip_sum(d)
            to_left = chip_sum(-d)
            coming[0].wait_recv()
            SR[d - 1, lo] = (to_right[:half_rows] + RR[d, lo].astype(jnp.float32)).astype(jnp.bfloat16)
            SR[d - 1, hi] = to_right[half_rows:].astype(jnp.bfloat16)
            coming[0] = ring_copy(SR.at[d - 1], RR.at[d - 1], 0, d, right)
            coming[1].wait_recv()
            SL[d - 1, hi] = (to_left[half_rows:] + RL[d, hi].astype(jnp.float32)).astype(jnp.bfloat16)
            SL[d - 1, lo] = to_left[:half_rows].astype(jnp.bfloat16)
            coming[1] = ring_copy(SL.at[d - 1], RL.at[d - 1], 1, d, left)
        else:
            coming[0].wait_recv()
            SR[d - 1] = (chip_sum(d) + RR[d].astype(jnp.float32)).astype(jnp.bfloat16)
            coming[0] = ring_copy(SR.at[d - 1], RR.at[d - 1], 0, d, right)
            coming[1].wait_recv()
            SL[d - 1] = (chip_sum(-d) + RL[d].astype(jnp.float32)).astype(jnp.bfloat16)
            coming[1] = ring_copy(SL.at[d - 1], RL.at[d - 1], 1, d, left)
    swap_done(0)
    total = chip_sum(0)
    coming[0].wait_recv()
    coming[1].wait_recv()
    total = total + RR[0].astype(jnp.float32) + RL[0].astype(jnp.float32)
    low, high = total[:, :width], total[:, width:]
    mine = jnp.where(a == 0, low, high)
    YS[...] = jnp.where(a == 0, high, low).astype(jnp.bfloat16)
    last = pltpu.make_async_remote_copy(
        src_ref=YS,
        dst_ref=YR,
        send_sem=ysend,
        recv_sem=yrecv,
        device_id=across,
        device_id_type=MESH,
    )
    last.start()
    for copy in pending + ring_copies:
        copy.wait_send()
    last.wait()
    out_ref[...] = (mine + YR[...].astype(jnp.float32)).astype(jnp.bfloat16)


def moe(u, meta, w_gate, w_up, w_down):
    n = lax.axis_size("exp")
    rings = n // 2
    half_ring = max(1, rings // 2)
    rows, width = u.shape
    full = 2 * width
    experts = meta.shape[0]
    per_chunk = 4 * rows
    sends = 4 * n + 8
    bf = jnp.bfloat16
    dma = pltpu.SemaphoreType.DMA
    return pl.pallas_call(
        functools.partial(moe_kernel, n),
        out_shape=jax.ShapeDtypeStruct((rows, width), bf),
        in_specs=[pl.BlockSpec(memory_space=pltpu.VMEM)] * 2
        + [pl.BlockSpec(memory_space=pl.ANY)] * 3,
        out_specs=pl.BlockSpec(memory_space=pltpu.VMEM),
        scratch_shapes=[
            pltpu.VMEM((full, width), bf),
            pltpu.VMEM((full, width), bf),
            pltpu.VMEM((width, full), bf),
            pltpu.VMEM((2, n, rows, width), bf),
            pltpu.VMEM((2, n, experts, 2 * rows), jnp.float32),
            pltpu.VMEM((per_chunk, width), bf),
            pltpu.VMEM((n, rows, full), bf),
            pltpu.VMEM((rings, rows, full), bf),
            pltpu.VMEM((half_ring, rows, full), bf),
            pltpu.VMEM((half_ring, rows, full), bf),
            pltpu.VMEM((half_ring, rows, full), bf),
            pltpu.VMEM((half_ring, rows, full), bf),
            pltpu.VMEM((rows, width), bf),
            pltpu.VMEM((rows, width), bf),
            dma((3,)),
            dma((sends,)),
            dma((2, n, 2)),
            dma((sends,)),
            dma((2, n)),
            dma((rings,)),
            dma((rings,)),
            dma((2, half_ring)),
            dma((2, half_ring)),
            dma,
            dma,
        ],
        compiler_params=pltpu.CompilerParams(
            collective_id=1, has_side_effects=True, vmem_limit_bytes=62 * 1024 * 1024
        ),
    )(u, meta, w_gate, w_up, w_down)


def ringed_experts(hidden, norm_gain, expert_ids, weight_codes, w_gate, w_up, w_down):
    rows = hidden.shape[0]
    squares = jnp.sum(hidden * hidden, axis=1)
    scaled = (hidden * norm_gain.astype(jnp.float32)[None, :]).astype(jnp.bfloat16)
    expert_count = w_gate.shape[0] * lax.axis_size("exp")
    shares = weight_codes.astype(jnp.float32)
    shares = shares / jnp.sum(shares, axis=1, keepdims=True)
    named = expert_ids[None, :, :] == jnp.arange(expert_count, dtype=jnp.int32)[:, None, None]
    by_expert = jnp.sum(jnp.where(named, shares[None], 0.0), axis=2)
    meta = jnp.concatenate(
        [by_expert, jnp.broadcast_to(squares[None, :], (expert_count, rows))], axis=1
    )
    return moe(scaled, meta, w_gate, w_up, w_down)


def routed_experts(hidden, norm_gain, expert_ids, weight_codes, w_gate, w_up, w_down):
    decode_row_count = hidden.shape[0]
    squares = lax.psum(jnp.sum(hidden * hidden, axis=1), "att")
    inverse = lax.rsqrt(squares / D + 1e-05)
    normed = (hidden * inverse[:, None] * norm_gain.astype(jnp.float32)[None, :]).astype(
        jnp.bfloat16
    )
    local_experts = w_gate.shape[0]
    expert_count = local_experts * lax.axis_size("exp")
    capacity = min(decode_row_count, max(2, 2 * decode_row_count * TOP // expert_count))
    flat_ids = expert_ids.reshape(-1)
    expert_hits = (flat_ids[:, None] == jnp.arange(expert_count, dtype=jnp.int32)[None, :]).astype(
        jnp.int32
    )
    earlier = jnp.cumsum(expert_hits, axis=0) - expert_hits
    position = jnp.sum(earlier * expert_hits, axis=1)
    slot_index = flat_ids * capacity + position
    placed = slot_index[None, :] == jnp.arange(expert_count * capacity, dtype=jnp.int32)[:, None]
    assign = jnp.any(placed.reshape(expert_count * capacity, decode_row_count, TOP), axis=2).astype(
        jnp.bfloat16
    )
    source_rows = lax.all_gather(normed, "att", axis=1, tiled=True)
    outgoing = jnp.dot(assign, source_rows, preferred_element_type=jnp.float32).astype(jnp.bfloat16)
    outgoing = outgoing.reshape(expert_count, capacity, -1)
    received = lax.all_to_all(outgoing, "exp", split_axis=0, concat_axis=0, tiled=True)
    senders = received.shape[0] // local_experts
    slot_count = received.shape[1]
    arranged = received.reshape(senders, local_experts, slot_count, received.shape[2])
    gate_sum = jnp.einsum("sekd,edf->sekf", arranged, w_gate, preferred_element_type=jnp.float32)
    up_sum = jnp.einsum("sekd,edf->sekf", arranged, w_up, preferred_element_type=jnp.float32)
    gate_sum = jnp.minimum(gate_sum, clamp_limit)
    up_sum = jnp.clip(up_sum, -clamp_limit, clamp_limit)
    active = (gate_sum * jax.nn.sigmoid(1.702 * gate_sum) * (up_sum + 1.0)).astype(jnp.bfloat16)
    partial_out = jnp.einsum("sekf,efd->sekd", active, w_down, preferred_element_type=jnp.float32)
    summed = lax.psum_scatter(
        partial_out.astype(jnp.bfloat16), "att", scatter_dimension=3, tiled=True
    )
    answer = lax.all_to_all(
        summed.reshape(senders * local_experts, slot_count, -1),
        "exp",
        split_axis=0,
        concat_axis=0,
        tiled=True,
    )
    flat_returned = answer.reshape(expert_count * capacity, -1)
    picked = flat_returned[slot_index].reshape(decode_row_count, TOP, -1).astype(jnp.float32)
    shares = weight_codes.astype(jnp.float32)
    shares = shares / jnp.sum(shares, axis=1, keepdims=True)
    mixture = jnp.sum(picked * shares[:, :, None], axis=1).astype(jnp.bfloat16)
    return mixture


def shards(
    queries,
    row_key_value,
    shared_context_cache,
    branch,
    sink_logits,
    w_out,
    residual,
    norm_gain,
    expert_ids,
    weight_codes,
    w_gate,
    w_up,
    w_down,
):
    decode_row_count = queries.shape[0]
    grouped_heads = queries.reshape(
        decode_row_count, KEY_VALUE_HEADS, QUERY_HEADS // KEY_VALUE_HEADS, HEAD_SIZE
    )
    partial_stats = local_partials(grouped_heads, shared_context_cache, branch)
    merged = combined_all(partial_stats, "att", merge_parts)
    attention = finish_attention(merged, grouped_heads, row_key_value, sink_logits)
    projected = jnp.dot(attention, w_out, preferred_element_type=jnp.float32)
    hidden = residual.astype(jnp.float32) + projected
    attended = hidden.astype(jnp.bfloat16)
    near = lax.axis_size("att") == 2 and lax.axis_size("exp") % 4 == 0 and w_gate.shape[0] == 1
    experts = ringed_experts if near else routed_experts
    mixture = experts(hidden, norm_gain, expert_ids, weight_codes, w_gate, w_up, w_down)
    return (attended, mixture)


def solution(mesh):
    placed = (
        P(("groups", "exp"), None),
        P(("groups", "exp"), None),
        P("groups", "att", None),
        P(("groups", "exp")),
        P(),
        P(None, "att"),
        P(("groups", "exp"), "att"),
        P("att"),
        P(("groups", "exp"), None),
        P(("groups", "exp"), None),
        P("exp", None, "att"),
        P("exp", None, "att"),
        P("exp", "att", None),
    )
    return jax.shard_map(
        shards,
        mesh=mesh,
        in_specs=placed,
        out_specs=(P(("groups", "exp"), "att"), P(("groups", "exp"), "att")),
        check_vma=False,
    )
```

```python
import functools

import jax
import jax.numpy as jnp
from jax import lax
from jax.experimental import pallas as pl
from jax.experimental.pallas import tpu as pltpu
from jax.sharding import PartitionSpec as P

D = 2880
QUERY_HEADS = 64
KEY_VALUE_HEADS = 8
HEAD_SIZE = 64
TOP = 4
SHARED_CONTEXTS = 2


MESH = pl.DeviceIdType.MESH
NT = (((1,), (1,)), ((), ()))
clamp_limit = 7.0


def combined_all(x, axis, combine):
    everything = jax.tree.map(
        lambda part, kind: lax.all_gather(part.astype(kind), axis),
        x,
        jax.tree.map(lambda a: jnp.bfloat16 if a.dtype == jnp.float32 else a.dtype, x),
    )

    def take(k):
        return jax.tree.map(lambda part, own: part[k].astype(own.dtype), everything, x)

    return lax.fori_loop(
        1, lax.axis_size(axis), lambda k, so_far: combine(so_far, take(k)), take(0)
    )


def merge_parts(first, second):
    first_max, first_total, first_out = first
    second_max, second_total, second_out = second
    joint_max = jnp.maximum(first_max, second_max)
    first_factor = jnp.exp(first_max - joint_max)
    second_factor = jnp.exp(second_max - joint_max)
    joint_total = first_total * first_factor + second_total * second_factor
    decode_row_count, head_count = first_max.shape
    joint_out = (
        first_out.reshape(decode_row_count, head_count, -1) * first_factor[:, :, None]
        + second_out.reshape(decode_row_count, head_count, -1) * second_factor[:, :, None]
    )
    return (joint_max, joint_total, joint_out.reshape(decode_row_count, -1))


def local_partials(grouped_heads, shared_context_cache, branch):
    decode_row_count = grouped_heads.shape[0]
    score_scale = HEAD_SIZE ** (-0.5)
    current = None
    for context_slot in range(SHARED_CONTEXTS):
        cached_key_block = shared_context_cache[
            context_slot, :, : KEY_VALUE_HEADS * HEAD_SIZE
        ].reshape(-1, KEY_VALUE_HEADS, HEAD_SIZE)
        cached_value_block = shared_context_cache[
            context_slot, :, KEY_VALUE_HEADS * HEAD_SIZE :
        ].reshape(-1, KEY_VALUE_HEADS, HEAD_SIZE)
        scores = (
            jnp.einsum(
                "rgqd,tgd->rgqt",
                grouped_heads,
                cached_key_block,
                preferred_element_type=jnp.float32,
            )
            * score_scale
        )
        local_max = jnp.max(scores, axis=-1)
        weights = jnp.exp(scores - local_max[..., None])
        local_total = jnp.sum(weights, axis=-1)
        local_out = jnp.einsum(
            "rgqt,tgd->rgqd",
            weights.astype(jnp.bfloat16),
            cached_value_block,
            preferred_element_type=jnp.float32,
        )
        if current is None:
            current = (local_max, local_total, local_out)
        else:
            chosen = branch == context_slot
            current = (
                jnp.where(chosen[:, None, None], local_max, current[0]),
                jnp.where(chosen[:, None, None], local_total, current[1]),
                jnp.where(chosen[:, None, None, None], local_out, current[2]),
            )
    return (
        current[0].reshape(decode_row_count, QUERY_HEADS),
        current[1].reshape(decode_row_count, QUERY_HEADS),
        current[2].reshape(decode_row_count, QUERY_HEADS * HEAD_SIZE),
    )


def finish_attention(merged, grouped_heads, row_key_value, sink_logits):
    decode_row_count = grouped_heads.shape[0]
    heads_per_group = QUERY_HEADS // KEY_VALUE_HEADS
    score_scale = HEAD_SIZE ** (-0.5)
    cache_max, cache_total, cache_out = merged
    row_own_keys = (
        row_key_value[:, : KEY_VALUE_HEADS * HEAD_SIZE]
        .reshape(decode_row_count, KEY_VALUE_HEADS, 1, HEAD_SIZE)
        .astype(jnp.float32)
    )
    row_own_values = (
        row_key_value[:, KEY_VALUE_HEADS * HEAD_SIZE :]
        .reshape(decode_row_count, KEY_VALUE_HEADS, 1, HEAD_SIZE)
        .astype(jnp.float32)
    )
    own_score = (
        jnp.sum(grouped_heads.astype(jnp.float32) * row_own_keys, axis=-1) * score_scale
    ).reshape(decode_row_count, QUERY_HEADS)
    row_own_values = jnp.broadcast_to(
        row_own_values, (decode_row_count, KEY_VALUE_HEADS, heads_per_group, HEAD_SIZE)
    ).reshape(decode_row_count, QUERY_HEADS, HEAD_SIZE)
    sink_row = sink_logits[None, :]
    peak = jnp.maximum(jnp.maximum(cache_max, own_score), sink_row)
    cache_factor = jnp.exp(cache_max - peak)
    own_factor = jnp.exp(own_score - peak)
    sink_factor = jnp.exp(sink_row - peak)
    denominator = cache_total * cache_factor + own_factor + sink_factor
    numerator = (
        cache_out.reshape(decode_row_count, QUERY_HEADS, HEAD_SIZE) * cache_factor[..., None]
        + own_factor[..., None] * row_own_values
    )
    return (
        (numerator / denominator[..., None])
        .reshape(decode_row_count, QUERY_HEADS * HEAD_SIZE)
        .astype(jnp.bfloat16)
    )

def layer_kernel(
    n,
    q_ref,
    kv_ref,
    branch_ref,
    sink_ref,
    residual_ref,
    gain_ref,
    share_ref,
    cache_hbm,
    wo_hbm,
    wg_hbm,
    wu_hbm,
    wd_hbm,
    attended_ref,
    out_ref,
    cache,
    wo,
    hidden_t,
    OS,
    OR,
    TS,
    TR,
    osend,
    orecv,
    tsend,
    trecv,
    wg,
    wu,
    wd,
    X,
    META,
    act_ref,
    P_ref,
    CS,
    SR,
    SL,
    RR,
    RL,
    YS,
    YR,
    wsem,
    xsend,
    xrecv,
    msend,
    mrecv,
    csend,
    crecv,
    rsend,
    rrecv,
    ysend,
    yrecv,
):
    rings = n // 2
    half_ring = rings // 2
    rows = residual_ref.shape[0]
    width = residual_ref.shape[1]
    half_rows = rows // 2
    experts = share_ref.shape[0]
    a = lax.axis_index("att")
    e = lax.axis_index("exp")
    z = e // 2
    c = e % 2

    def at(offset):
        return lax.rem(z + offset + rings, rings)

    def lane(offset):
        return at(offset) * 2 + c

    right = {"exp": lane(1)}
    left = {"exp": lane(-1)}
    mate = {"exp": z * 2 + 1 - c}
    across = {"att": 1 - a}

    cache_load = pltpu.make_async_copy(cache_hbm, cache, wsem.at[3])
    cache_load.start()
    wo_load = pltpu.make_async_copy(wo_hbm, wo, wsem.at[4])
    wo_load.start()
    loads = [
        pltpu.make_async_copy(wg_hbm.at[0], wg, wsem.at[0]),
        pltpu.make_async_copy(wu_hbm.at[0], wu, wsem.at[1]),
        pltpu.make_async_copy(wd_hbm.at[0], wd, wsem.at[2]),
    ]
    for load in loads:
        load.start()

    barrier = pltpu.get_barrier_semaphore()
    for target in (right, left, mate, across):
        pl.semaphore_signal(barrier, inc=1, device_id=target, device_id_type=MESH)
    pl.semaphore_wait(barrier, 4)
    eye = lax.broadcasted_iota(jnp.int32, (rows, rows), 0) == lax.broadcasted_iota(
        jnp.int32, (rows, rows), 1
    )

    per = QUERY_HEADS // KEY_VALUE_HEADS
    columns = per * rows
    pair = 2 * HEAD_SIZE
    pairs = KEY_VALUE_HEADS // 2
    kv_width = KEY_VALUE_HEADS * HEAD_SIZE
    second_context = branch_ref[...] == 1

    def transposed_queries(g2):
        start = pl.multiple_of(g2 * 2 * per * HEAD_SIZE, 128)
        block = q_ref[:, pl.ds(start, 2 * per * HEAD_SIZE)].astype(jnp.float32).T
        block = block * HEAD_SIZE ** (-0.5)

        def head(k):
            return block[k * HEAD_SIZE : (k + 1) * HEAD_SIZE]

        return [
            jnp.concatenate([head(j * per + h) for h in range(per)], axis=1) for j in range(2)
        ]

    def parts_copies(g2):
        return (
            pltpu.make_async_remote_copy(
                src_ref=OS.at[g2],
                dst_ref=OR.at[g2],
                send_sem=osend.at[g2],
                recv_sem=orecv.at[g2],
                device_id=across,
                device_id_type=MESH,
            ),
            pltpu.make_async_remote_copy(
                src_ref=TS.at[g2],
                dst_ref=TR.at[g2],
                send_sem=tsend.at[g2],
                recv_sem=trecv.at[g2],
                device_id=across,
                device_id_type=MESH,
            ),
        )

    cache_load.wait()

    @pl.loop(0, pairs)
    def _(g2):
        heads_t = transposed_queries(g2)
        key_cols = pl.ds(pl.multiple_of(g2 * pair, 128), pair)
        value_cols = pl.ds(pl.multiple_of(kv_width + g2 * pair, 128), pair)
        keys = jnp.concatenate([cache[0, :, key_cols], cache[1, :, key_cols]], axis=1)
        values_t = [cache[k, :, value_cols].T for k in range(2)]
        for j in range(2):
            q = heads_t[j]
            none = jnp.zeros_like(q)
            first_q = jnp.where(second_context, 0.0, q)
            second_q = jnp.where(second_context, q, 0.0)
            stack = [first_q, none, second_q, none] if j == 0 else [none, first_q, none, second_q]
            stacked = jnp.concatenate(stack, axis=0).astype(jnp.bfloat16)
            scores = jnp.dot(keys, stacked, preferred_element_type=jnp.float32)
            top = jnp.max(scores, axis=0, keepdims=True)
            weights = jnp.exp(scores - top)
            total = jnp.sum(weights, axis=0, keepdims=True)
            own_rows = slice(j * HEAD_SIZE, (j + 1) * HEAD_SIZE)
            values = jnp.concatenate([v[own_rows] for v in values_t], axis=0)
            out = jnp.dot(
                values, weights.astype(jnp.bfloat16), preferred_element_type=jnp.float32
            )
            out = jnp.where(second_context, out[HEAD_SIZE:], out[:HEAD_SIZE])
            OS[g2, own_rows, :] = out.astype(jnp.bfloat16)
            TS[g2, 2 * j : 2 * j + 1, :] = top
            TS[g2, 2 * j + 1 : 2 * j + 2, :] = total
        for copy in parts_copies(g2):
            copy.start()

    hidden_t[...] = jnp.zeros_like(hidden_t)
    wo_load.wait()

    @pl.loop(0, pairs)
    def _(g2):
        heads_t = transposed_queries(g2)
        key_cols = pl.ds(pl.multiple_of(g2 * pair, 128), pair)
        value_cols = pl.ds(pl.multiple_of(kv_width + g2 * pair, 128), pair)
        own_keys = kv_ref[:, key_cols].astype(jnp.float32).T
        own_values = kv_ref[:, value_cols].astype(jnp.float32).T
        sinks = sink_ref[g2]
        for copy in parts_copies(g2):
            copy.wait()
        mine, theirs = TS[g2], TR[g2]
        stacked = []
        for j in range(2):
            own_rows = slice(j * HEAD_SIZE, (j + 1) * HEAD_SIZE)
            own_key = jnp.concatenate([own_keys[own_rows]] * per, axis=1)
            own_value = jnp.concatenate([own_values[own_rows]] * per, axis=1)
            own_score = jnp.sum(heads_t[j] * own_key, axis=0, keepdims=True)
            sink = sinks[j : j + 1]
            top_a, top_b = mine[2 * j : 2 * j + 1], theirs[2 * j : 2 * j + 1]
            peak = jnp.maximum(jnp.maximum(top_a, top_b), jnp.maximum(own_score, sink))
            factor_a = jnp.exp(top_a - peak)
            factor_b = jnp.exp(top_b - peak)
            own_factor = jnp.exp(own_score - peak)
            denominator = (
                mine[2 * j + 1 : 2 * j + 2] * factor_a
                + theirs[2 * j + 1 : 2 * j + 2] * factor_b
                + own_factor
                + jnp.exp(sink - peak)
            )
            out = (
                OS[g2, own_rows, :].astype(jnp.float32) * factor_a
                + OR[g2, own_rows, :].astype(jnp.float32) * factor_b
                + own_factor * own_value
            ) / denominator
            stacked += [out[:, h * rows : (h + 1) * rows] for h in range(per)]
        attention_t = jnp.concatenate(stacked, axis=0).astype(jnp.bfloat16)
        cols = pl.ds(pl.multiple_of(g2 * 2 * per * HEAD_SIZE, 128), 2 * per * HEAD_SIZE)
        hidden_t[...] += jnp.dot(wo[:, cols], attention_t, preferred_element_type=jnp.float32)

    hidden = hidden_t[...].T + residual_ref[...].astype(jnp.float32)
    attended_ref[...] = hidden.astype(jnp.bfloat16)
    squares = jnp.sum(hidden * hidden, axis=1, keepdims=True)
    squares = jnp.sum(
        jnp.where(eye, jnp.broadcast_to(squares, (rows, rows)), 0.0), axis=0, keepdims=True
    )
    META[a, e] = jnp.concatenate(
        [share_ref[...], jnp.broadcast_to(squares, (experts, rows))], axis=1
    )
    X[a, e] = (hidden * gain_ref[...].astype(jnp.float32)).astype(jnp.bfloat16)

    pending = []
    counter = [0]

    def send(src_x, src_m, h, idx, target, part=None):
        k = counter[0]
        counter[0] += 1
        if part is None:
            dst_x, slot = X.at[h, idx], 0
        else:
            dst_x, slot = X.at[h, idx, pl.ds(part * half_rows, half_rows)], part
        x_copy = pltpu.make_async_remote_copy(
            src_ref=src_x,
            dst_ref=dst_x,
            send_sem=xsend.at[k],
            recv_sem=xrecv.at[h, idx, slot],
            device_id=target,
            device_id_type=MESH,
        )
        x_copy.start()
        pending.append(x_copy)
        if part is None or part == 0:
            m_copy = pltpu.make_async_remote_copy(
                src_ref=src_m,
                dst_ref=META.at[h, idx],
                send_sem=msend.at[k],
                recv_sem=mrecv.at[h, idx],
                device_id=target,
                device_id_type=MESH,
            )
            m_copy.start()
            pending.append(m_copy)

    def arrived(h, idx, part=None):
        if part is None:
            ref, slot = X.at[h, idx], 0
        else:
            ref, slot = X.at[h, idx, pl.ds(part * half_rows, half_rows)], part
        pltpu.make_async_remote_copy(
            src_ref=ref,
            dst_ref=ref,
            send_sem=xsend.at[0],
            recv_sem=xrecv.at[h, idx, slot],
            device_id=mate,
            device_id_type=MESH,
        ).wait_recv()
        if part is None or part == 0:
            pltpu.make_async_remote_copy(
                src_ref=META.at[h, idx],
                dst_ref=META.at[h, idx],
                send_sem=msend.at[0],
                recv_sem=mrecv.at[h, idx],
                device_id=mate,
                device_id_type=MESH,
            ).wait_recv()

    halves = (a, 1 - a)
    for target in (across, right, left, mate):
        send(X.at[a, e], META.at[a, e], a, e, target)
    arrived(1 - a, e)
    own = (1 - a, e)
    for target in (right, left, mate):
        send(X.at[own], META.at[own], 1 - a, e, target)

    def forward(step, h):
        from_left, from_right = lane(-step), lane(step)
        if step < half_ring:
            last = step + 1 == half_ring
            arrived(h, from_left)
            if last:
                lo = pl.ds(0, half_rows)
                send(X.at[h, from_left, lo], META.at[h, from_left], h, from_left, right, 0)
            else:
                send(X.at[h, from_left], META.at[h, from_left], h, from_left, right)
            arrived(h, from_right)
            if last:
                hi = pl.ds(half_rows, half_rows)
                send(X.at[h, from_right, hi], None, h, from_right, left, 1)
            else:
                send(X.at[h, from_right], META.at[h, from_right], h, from_right, left)
            send(X.at[h, from_left], META.at[h, from_left], h, from_left, mate)
            send(X.at[h, from_right], META.at[h, from_right], h, from_right, mate)
        else:
            arrived(h, from_left, 0)
            arrived(h, from_left, 1)
            send(X.at[h, from_left], META.at[h, from_left], h, from_left, mate)

    def mates(step, h):
        arrived(h, at(-step) * 2 + 1 - c)
        if 0 < step < half_ring:
            arrived(h, at(step) * 2 + 1 - c)

    def upright(row):
        return jnp.sum(jnp.where(eye, jnp.broadcast_to(row, (rows, rows)), 0.0), axis=1, keepdims=True)

    def run_chunk(offsets):
        blocks = [at(o) * 2 + k for o in offsets for k in range(2)]
        count = len(blocks) * rows
        x = jnp.concatenate(
            [jnp.concatenate([X[0, b], X[1, b]], axis=1) for b in blocks], axis=0
        )
        shares, inverses = [], []
        pick = lax.broadcasted_iota(jnp.int32, (experts, 2 * rows), 0) == e
        for b in blocks:
            squares = META[0, b][0:1, rows : 2 * rows] + META[1, b][0:1, rows : 2 * rows]
            inverses.append(upright(lax.rsqrt(squares / (2 * width) + 1e-05)))
            mine = jnp.sum(jnp.where(pick, META[0, b], 0.0), axis=0, keepdims=True)
            shares.append(upright(mine[:, :rows]))
        inverse = jnp.concatenate(inverses, axis=0)
        share = jnp.concatenate(shares, axis=0)

        def first(start, size):
            cols = pl.ds(start, size)
            g = lax.dot_general(x, wg[cols, :], NT, preferred_element_type=jnp.float32)
            u = lax.dot_general(x, wu[cols, :], NT, preferred_element_type=jnp.float32)
            g = jnp.minimum(g * inverse, clamp_limit)
            u = jnp.clip(u * inverse, -clamp_limit, clamp_limit)
            act_ref[:, cols] = (g * jax.nn.sigmoid(1.702 * g) * (u + 1.0)).astype(jnp.bfloat16)

        def second(start, size):
            cols = pl.ds(start, size)
            y = jnp.dot(act_ref[...], wd[:, cols], preferred_element_type=jnp.float32)
            y = (y * share).astype(jnp.bfloat16)
            for k, b in enumerate(blocks):
                P_ref[b, :, cols] = y[k * rows : (k + 1) * rows]

        def tiled(body, total, tile):
            whole_tiles = total // tile

            @pl.loop(0, whole_tiles)
            def _(i):
                body(pl.multiple_of(i * tile, tile), tile)

            if total % tile:
                body(whole_tiles * tile, total % tile)

        return tiled, first, second

    order = [0]
    for s in range(1, half_ring):
        order += [-s, s]
    order += [half_ring]
    chunks = [order[k : k + 2] for k in range(0, len(order), 2)]

    c_copies = []

    def swap(offset):
        dest = at(offset)
        k = offset % rings
        copy = pltpu.make_async_remote_copy(
            src_ref=P_ref.at[dest * 2 + 1 - c],
            dst_ref=CS.at[dest],
            send_sem=csend.at[k],
            recv_sem=crecv.at[dest],
            device_id=mate,
            device_id_type=MESH,
        )
        copy.start()
        return copy

    for step in range(1, half_ring + 1):
        for h in halves:
            forward(step, h)
    for step in range(0, half_ring + 1):
        for h in halves:
            mates(step, h)
    loads[0].wait()
    loads[1].wait()
    loads[2].wait()
    swaps = {}
    for offsets in chunks[::-1]:
        tiled, first, second = run_chunk(offsets)
        tiled(first, width, 256)
        tiled(second, 2 * width, 256)
        for o in offsets:
            swaps[o % rings] = swap(o)

    def chip_sum(offset):
        dest = at(offset)
        return P_ref[dest * 2 + c].astype(jnp.float32) + CS[dest].astype(jnp.float32)

    ring_copies = []

    def ring_copy(src, dst, k, d, target):
        copy = pltpu.make_async_remote_copy(
            src_ref=src,
            dst_ref=dst,
            send_sem=rsend.at[k, d - 1],
            recv_sem=rrecv.at[k, d - 1],
            device_id=target,
            device_id_type=MESH,
        )
        copy.start()
        ring_copies.append(copy)
        return copy

    coming = {}
    lo = pl.ds(0, half_rows)
    hi = pl.ds(half_rows, half_rows)
    swapped = set()

    def swap_done(offset):
        k = offset % rings
        if k not in swapped:
            swapped.add(k)
            swaps[k].wait()

    for d in range(half_ring, 0, -1):
        swap_done(d)
        swap_done(-d)
        if d == half_ring:
            total = chip_sum(d).astype(jnp.bfloat16)
            SR[d - 1, lo] = total[:half_rows]
            SL[d - 1, hi] = total[half_rows:]
            coming[0] = ring_copy(SR.at[d - 1, lo], RR.at[d - 1, lo], 0, d, right)
            coming[1] = ring_copy(SL.at[d - 1, hi], RL.at[d - 1, hi], 1, d, left)
            continue
        if d + 1 == half_ring:
            to_right = chip_sum(d)
            to_left = chip_sum(-d)
            coming[0].wait_recv()
            SR[d - 1, lo] = (to_right[:half_rows] + RR[d, lo].astype(jnp.float32)).astype(jnp.bfloat16)
            SR[d - 1, hi] = to_right[half_rows:].astype(jnp.bfloat16)
            coming[0] = ring_copy(SR.at[d - 1], RR.at[d - 1], 0, d, right)
            coming[1].wait_recv()
            SL[d - 1, hi] = (to_left[half_rows:] + RL[d, hi].astype(jnp.float32)).astype(jnp.bfloat16)
            SL[d - 1, lo] = to_left[:half_rows].astype(jnp.bfloat16)
            coming[1] = ring_copy(SL.at[d - 1], RL.at[d - 1], 1, d, left)
        else:
            coming[0].wait_recv()
            SR[d - 1] = (chip_sum(d) + RR[d].astype(jnp.float32)).astype(jnp.bfloat16)
            coming[0] = ring_copy(SR.at[d - 1], RR.at[d - 1], 0, d, right)
            coming[1].wait_recv()
            SL[d - 1] = (chip_sum(-d) + RL[d].astype(jnp.float32)).astype(jnp.bfloat16)
            coming[1] = ring_copy(SL.at[d - 1], RL.at[d - 1], 1, d, left)
    swap_done(0)
    total = chip_sum(0)
    coming[0].wait_recv()
    coming[1].wait_recv()
    total = total + RR[0].astype(jnp.float32) + RL[0].astype(jnp.float32)
    low, high = total[:, :width], total[:, width:]
    mine = jnp.where(a == 0, low, high)
    YS[...] = jnp.where(a == 0, high, low).astype(jnp.bfloat16)
    last = pltpu.make_async_remote_copy(
        src_ref=YS,
        dst_ref=YR,
        send_sem=ysend,
        recv_sem=yrecv,
        device_id=across,
        device_id_type=MESH,
    )
    last.start()
    for copy in pending + ring_copies:
        copy.wait_send()
    last.wait()
    out_ref[...] = (mine + YR[...].astype(jnp.float32)).astype(jnp.bfloat16)


def layer(
    queries, row_key_value, cache, branch, sinks, w_out, residual, gain, by_expert, w_gate, w_up, w_down
):
    n = lax.axis_size("exp")
    rings = n // 2
    half_ring = max(1, rings // 2)
    rows, width = residual.shape
    per = QUERY_HEADS // KEY_VALUE_HEADS
    pairs = KEY_VALUE_HEADS // 2
    full = 2 * width
    experts = by_expert.shape[0]
    per_chunk = 4 * rows
    sends = 4 * n + 8
    bf = jnp.bfloat16
    dma = pltpu.SemaphoreType.DMA
    return pl.pallas_call(
        functools.partial(layer_kernel, n),
        out_shape=[jax.ShapeDtypeStruct((rows, width), bf)] * 2,
        in_specs=[pl.BlockSpec(memory_space=pltpu.VMEM)] * 7
        + [pl.BlockSpec(memory_space=pl.ANY)] * 5,
        out_specs=[pl.BlockSpec(memory_space=pltpu.VMEM)] * 2,
        scratch_shapes=[
            pltpu.VMEM(cache.shape, bf),
            pltpu.VMEM((width, QUERY_HEADS * HEAD_SIZE), bf),
            pltpu.VMEM((width, rows), jnp.float32),
            pltpu.VMEM((pairs, 2 * HEAD_SIZE, per * rows), bf),
            pltpu.VMEM((pairs, 2 * HEAD_SIZE, per * rows), bf),
            pltpu.VMEM((pairs, 8, per * rows), jnp.float32),
            pltpu.VMEM((pairs, 8, per * rows), jnp.float32),
            dma((pairs,)),
            dma((pairs,)),
            dma((pairs,)),
            dma((pairs,)),
            pltpu.VMEM((width, full), bf),
            pltpu.VMEM((width, full), bf),
            pltpu.VMEM((width, full), bf),
            pltpu.VMEM((2, n, rows, width), bf),
            pltpu.VMEM((2, n, experts, 2 * rows), jnp.float32),
            pltpu.VMEM((per_chunk, width), bf),
            pltpu.VMEM((n, rows, full), bf),
            pltpu.VMEM((rings, rows, full), bf),
            pltpu.VMEM((half_ring, rows, full), bf),
            pltpu.VMEM((half_ring, rows, full), bf),
            pltpu.VMEM((half_ring, rows, full), bf),
            pltpu.VMEM((half_ring, rows, full), bf),
            pltpu.VMEM((rows, width), bf),
            pltpu.VMEM((rows, width), bf),
            dma((5,)),
            dma((sends,)),
            dma((2, n, 2)),
            dma((sends,)),
            dma((2, n)),
            dma((rings,)),
            dma((rings,)),
            dma((2, half_ring)),
            dma((2, half_ring)),
            dma,
            dma,
        ],
        compiler_params=pltpu.CompilerParams(
            collective_id=1, has_side_effects=True, vmem_limit_bytes=62 * 1024 * 1024
        ),
    )(
        queries,
        row_key_value,
        jnp.tile(branch, per)[None, :],
        jnp.repeat(sinks, rows).reshape(pairs, 2, per * rows),
        residual,
        gain[None, :],
        by_expert,
        cache,
        w_out.T,
        jnp.swapaxes(w_gate, 1, 2),
        jnp.swapaxes(w_up, 1, 2),
        w_down,
    )


def share_table(expert_ids, weight_codes, expert_count):
    shares = weight_codes.astype(jnp.float32)
    shares = shares / jnp.sum(shares, axis=1, keepdims=True)
    named = expert_ids[None, :, :] == jnp.arange(expert_count, dtype=jnp.int32)[:, None, None]
    return jnp.sum(jnp.where(named, shares[None], 0.0), axis=2)


def routed_experts(hidden, norm_gain, expert_ids, weight_codes, w_gate, w_up, w_down):
    decode_row_count = hidden.shape[0]
    squares = lax.psum(jnp.sum(hidden * hidden, axis=1), "att")
    inverse = lax.rsqrt(squares / D + 1e-05)
    normed = (hidden * inverse[:, None] * norm_gain.astype(jnp.float32)[None, :]).astype(
        jnp.bfloat16
    )
    local_experts = w_gate.shape[0]
    expert_count = local_experts * lax.axis_size("exp")
    capacity = min(decode_row_count, max(2, 2 * decode_row_count * TOP // expert_count))
    flat_ids = expert_ids.reshape(-1)
    expert_hits = (flat_ids[:, None] == jnp.arange(expert_count, dtype=jnp.int32)[None, :]).astype(
        jnp.int32
    )
    earlier = jnp.cumsum(expert_hits, axis=0) - expert_hits
    position = jnp.sum(earlier * expert_hits, axis=1)
    slot_index = flat_ids * capacity + position
    placed = slot_index[None, :] == jnp.arange(expert_count * capacity, dtype=jnp.int32)[:, None]
    assign = jnp.any(placed.reshape(expert_count * capacity, decode_row_count, TOP), axis=2).astype(
        jnp.bfloat16
    )
    source_rows = lax.all_gather(normed, "att", axis=1, tiled=True)
    outgoing = jnp.dot(assign, source_rows, preferred_element_type=jnp.float32).astype(jnp.bfloat16)
    outgoing = outgoing.reshape(expert_count, capacity, -1)
    received = lax.all_to_all(outgoing, "exp", split_axis=0, concat_axis=0, tiled=True)
    senders = received.shape[0] // local_experts
    slot_count = received.shape[1]
    arranged = received.reshape(senders, local_experts, slot_count, received.shape[2])
    gate_sum = jnp.einsum("sekd,edf->sekf", arranged, w_gate, preferred_element_type=jnp.float32)
    up_sum = jnp.einsum("sekd,edf->sekf", arranged, w_up, preferred_element_type=jnp.float32)
    gate_sum = jnp.minimum(gate_sum, clamp_limit)
    up_sum = jnp.clip(up_sum, -clamp_limit, clamp_limit)
    active = (gate_sum * jax.nn.sigmoid(1.702 * gate_sum) * (up_sum + 1.0)).astype(jnp.bfloat16)
    partial_out = jnp.einsum("sekf,efd->sekd", active, w_down, preferred_element_type=jnp.float32)
    summed = lax.psum_scatter(
        partial_out.astype(jnp.bfloat16), "att", scatter_dimension=3, tiled=True
    )
    answer = lax.all_to_all(
        summed.reshape(senders * local_experts, slot_count, -1),
        "exp",
        split_axis=0,
        concat_axis=0,
        tiled=True,
    )
    flat_returned = answer.reshape(expert_count * capacity, -1)
    picked = flat_returned[slot_index].reshape(decode_row_count, TOP, -1).astype(jnp.float32)
    shares = weight_codes.astype(jnp.float32)
    shares = shares / jnp.sum(shares, axis=1, keepdims=True)
    mixture = jnp.sum(picked * shares[:, :, None], axis=1).astype(jnp.bfloat16)
    return mixture


def shards(
    queries,
    row_key_value,
    shared_context_cache,
    branch,
    sink_logits,
    w_out,
    residual,
    norm_gain,
    expert_ids,
    weight_codes,
    w_gate,
    w_up,
    w_down,
):
    near = lax.axis_size("att") == 2 and lax.axis_size("exp") % 4 == 0 and w_gate.shape[0] == 1
    if near:
        return layer(
            queries,
            row_key_value,
            shared_context_cache,
            branch,
            sink_logits,
            w_out,
            residual,
            norm_gain,
            share_table(expert_ids, weight_codes, w_gate.shape[0] * lax.axis_size("exp")),
            w_gate,
            w_up,
            w_down,
        )
    decode_row_count = queries.shape[0]
    grouped_heads = queries.reshape(
        decode_row_count, KEY_VALUE_HEADS, QUERY_HEADS // KEY_VALUE_HEADS, HEAD_SIZE
    )
    partial_stats = local_partials(grouped_heads, shared_context_cache, branch)
    merged = combined_all(partial_stats, "att", merge_parts)
    attention = finish_attention(merged, grouped_heads, row_key_value, sink_logits)
    projected = jnp.dot(attention, w_out, preferred_element_type=jnp.float32)
    hidden = residual.astype(jnp.float32) + projected
    attended = hidden.astype(jnp.bfloat16)
    mixture = routed_experts(
        hidden, norm_gain, expert_ids, weight_codes, w_gate, w_up, w_down
    )
    return (attended, mixture)


def solution(mesh):
    placed = (
        P(("groups", "exp"), None),
        P(("groups", "exp"), None),
        P("groups", "att", None),
        P(("groups", "exp")),
        P(),
        P(None, "att"),
        P(("groups", "exp"), "att"),
        P("att"),
        P(("groups", "exp"), None),
        P(("groups", "exp"), None),
        P("exp", None, "att"),
        P("exp", None, "att"),
        P("exp", "att", None),
    )
    return jax.shard_map(
        shards,
        mesh=mesh,
        in_specs=placed,
        out_specs=(P(("groups", "exp"), "att"), P(("groups", "exp"), "att")),
        check_vma=False,
    )
```

```python
import functools

import jax
import jax.numpy as jnp
from jax import lax
from jax.experimental import pallas as pl
from jax.experimental.pallas import tpu as pltpu
from jax.sharding import PartitionSpec as P

D = 2880
QUERY_HEADS = 64
KEY_VALUE_HEADS = 8
HEAD_SIZE = 64
TOP = 4
SHARED_CONTEXTS = 2


MESH = pl.DeviceIdType.MESH
NT = (((1,), (1,)), ((), ()))
clamp_limit = 7.0


def combined_all(x, axis, combine):
    everything = jax.tree.map(
        lambda part, kind: lax.all_gather(part.astype(kind), axis),
        x,
        jax.tree.map(lambda a: jnp.bfloat16 if a.dtype == jnp.float32 else a.dtype, x),
    )

    def take(k):
        return jax.tree.map(lambda part, own: part[k].astype(own.dtype), everything, x)

    return lax.fori_loop(
        1, lax.axis_size(axis), lambda k, so_far: combine(so_far, take(k)), take(0)
    )


def merge_parts(first, second):
    first_max, first_total, first_out = first
    second_max, second_total, second_out = second
    joint_max = jnp.maximum(first_max, second_max)
    first_factor = jnp.exp(first_max - joint_max)
    second_factor = jnp.exp(second_max - joint_max)
    joint_total = first_total * first_factor + second_total * second_factor
    decode_row_count, head_count = first_max.shape
    joint_out = (
        first_out.reshape(decode_row_count, head_count, -1) * first_factor[:, :, None]
        + second_out.reshape(decode_row_count, head_count, -1) * second_factor[:, :, None]
    )
    return (joint_max, joint_total, joint_out.reshape(decode_row_count, -1))


def local_partials(grouped_heads, shared_context_cache, branch):
    decode_row_count = grouped_heads.shape[0]
    score_scale = HEAD_SIZE ** (-0.5)
    current = None
    for context_slot in range(SHARED_CONTEXTS):
        cached_key_block = shared_context_cache[
            context_slot, :, : KEY_VALUE_HEADS * HEAD_SIZE
        ].reshape(-1, KEY_VALUE_HEADS, HEAD_SIZE)
        cached_value_block = shared_context_cache[
            context_slot, :, KEY_VALUE_HEADS * HEAD_SIZE :
        ].reshape(-1, KEY_VALUE_HEADS, HEAD_SIZE)
        scores = (
            jnp.einsum(
                "rgqd,tgd->rgqt",
                grouped_heads,
                cached_key_block,
                preferred_element_type=jnp.float32,
            )
            * score_scale
        )
        local_max = jnp.max(scores, axis=-1)
        weights = jnp.exp(scores - local_max[..., None])
        local_total = jnp.sum(weights, axis=-1)
        local_out = jnp.einsum(
            "rgqt,tgd->rgqd",
            weights.astype(jnp.bfloat16),
            cached_value_block,
            preferred_element_type=jnp.float32,
        )
        if current is None:
            current = (local_max, local_total, local_out)
        else:
            chosen = branch == context_slot
            current = (
                jnp.where(chosen[:, None, None], local_max, current[0]),
                jnp.where(chosen[:, None, None], local_total, current[1]),
                jnp.where(chosen[:, None, None, None], local_out, current[2]),
            )
    return (
        current[0].reshape(decode_row_count, QUERY_HEADS),
        current[1].reshape(decode_row_count, QUERY_HEADS),
        current[2].reshape(decode_row_count, QUERY_HEADS * HEAD_SIZE),
    )


def finish_attention(merged, grouped_heads, row_key_value, sink_logits):
    decode_row_count = grouped_heads.shape[0]
    heads_per_group = QUERY_HEADS // KEY_VALUE_HEADS
    score_scale = HEAD_SIZE ** (-0.5)
    cache_max, cache_total, cache_out = merged
    row_own_keys = (
        row_key_value[:, : KEY_VALUE_HEADS * HEAD_SIZE]
        .reshape(decode_row_count, KEY_VALUE_HEADS, 1, HEAD_SIZE)
        .astype(jnp.float32)
    )
    row_own_values = (
        row_key_value[:, KEY_VALUE_HEADS * HEAD_SIZE :]
        .reshape(decode_row_count, KEY_VALUE_HEADS, 1, HEAD_SIZE)
        .astype(jnp.float32)
    )
    own_score = (
        jnp.sum(grouped_heads.astype(jnp.float32) * row_own_keys, axis=-1) * score_scale
    ).reshape(decode_row_count, QUERY_HEADS)
    row_own_values = jnp.broadcast_to(
        row_own_values, (decode_row_count, KEY_VALUE_HEADS, heads_per_group, HEAD_SIZE)
    ).reshape(decode_row_count, QUERY_HEADS, HEAD_SIZE)
    sink_row = sink_logits[None, :]
    peak = jnp.maximum(jnp.maximum(cache_max, own_score), sink_row)
    cache_factor = jnp.exp(cache_max - peak)
    own_factor = jnp.exp(own_score - peak)
    sink_factor = jnp.exp(sink_row - peak)
    denominator = cache_total * cache_factor + own_factor + sink_factor
    numerator = (
        cache_out.reshape(decode_row_count, QUERY_HEADS, HEAD_SIZE) * cache_factor[..., None]
        + own_factor[..., None] * row_own_values
    )
    return (
        (numerator / denominator[..., None])
        .reshape(decode_row_count, QUERY_HEADS * HEAD_SIZE)
        .astype(jnp.bfloat16)
    )

def layer_kernel(
    n,
    q_ref,
    kv_ref,
    branch_ref,
    sink_ref,
    residual_ref,
    gain_ref,
    share_ref,
    cache_hbm,
    wo_hbm,
    wg_hbm,
    wu_hbm,
    wd_hbm,
    attended_ref,
    out_ref,
    cache,
    wo,
    hidden_t,
    OS,
    OR,
    TS,
    TR,
    osend,
    orecv,
    tsend,
    trecv,
    wg,
    wu,
    wd,
    X,
    META,
    act_ref,
    P_ref,
    CS,
    KEEP,
    ZS,
    ZR,
    YS,
    YR,
    wsem,
    xsend,
    xrecv,
    msend,
    mrecv,
    csend,
    crecv,
    rsend,
    rrecv,
    ysend,
    yrecv,
):
    rings = n // 2
    rows = residual_ref.shape[0]
    width = residual_ref.shape[1]
    experts = share_ref.shape[0]
    a = lax.axis_index("att")
    e = lax.axis_index("exp")
    z = e // 2
    c = e % 2

    pair_count = rings // 2
    side = z % 2
    groups_of_chips = []
    for k in range(pair_count):
        base = lax.rem(z // 2 + k, pair_count) * 2
        groups_of_chips.append([base + side, base + 1 - side] if k == 0 else [base + 1 - side, base + side])
    others = [chip for group in groups_of_chips for chip in group][1:]
    mate = {"exp": z * 2 + 1 - c}
    across = {"att": 1 - a}

    cache_load = pltpu.make_async_copy(cache_hbm, cache, wsem.at[3])
    cache_load.start()
    wo_load = pltpu.make_async_copy(wo_hbm, wo, wsem.at[4])
    wo_load.start()
    loads = [
        pltpu.make_async_copy(wg_hbm.at[0], wg, wsem.at[0]),
        pltpu.make_async_copy(wu_hbm.at[0], wu, wsem.at[1]),
        pltpu.make_async_copy(wd_hbm.at[0], wd, wsem.at[2]),
    ]
    for load in loads:
        load.start()

    barrier = pltpu.get_barrier_semaphore()
    for target in [mate, across] + [{"exp": chip * 2 + c} for chip in others]:
        pl.semaphore_signal(barrier, inc=1, device_id=target, device_id_type=MESH)
    pl.semaphore_wait(barrier, rings + 1)
    eye = lax.broadcasted_iota(jnp.int32, (rows, rows), 0) == lax.broadcasted_iota(
        jnp.int32, (rows, rows), 1
    )

    per = QUERY_HEADS // KEY_VALUE_HEADS
    columns = per * rows
    pair = 2 * HEAD_SIZE
    pairs = KEY_VALUE_HEADS // 2
    kv_width = KEY_VALUE_HEADS * HEAD_SIZE
    second_context = branch_ref[...] == 1

    def transposed_queries(g2):
        start = pl.multiple_of(g2 * 2 * per * HEAD_SIZE, 128)
        block = q_ref[:, pl.ds(start, 2 * per * HEAD_SIZE)].astype(jnp.float32).T
        block = block * HEAD_SIZE ** (-0.5)

        def head(k):
            return block[k * HEAD_SIZE : (k + 1) * HEAD_SIZE]

        return [
            jnp.concatenate([head(j * per + h) for h in range(per)], axis=1) for j in range(2)
        ]

    def parts_copies(g2):
        return (
            pltpu.make_async_remote_copy(
                src_ref=OS.at[g2],
                dst_ref=OR.at[g2],
                send_sem=osend.at[g2],
                recv_sem=orecv.at[g2],
                device_id=across,
                device_id_type=MESH,
            ),
            pltpu.make_async_remote_copy(
                src_ref=TS.at[g2],
                dst_ref=TR.at[g2],
                send_sem=tsend.at[g2],
                recv_sem=trecv.at[g2],
                device_id=across,
                device_id_type=MESH,
            ),
        )

    cache_load.wait()

    @pl.loop(0, pairs)
    def _(g2):
        heads_t = transposed_queries(g2)
        key_cols = pl.ds(pl.multiple_of(g2 * pair, 128), pair)
        value_cols = pl.ds(pl.multiple_of(kv_width + g2 * pair, 128), pair)
        keys = jnp.concatenate([cache[0, :, key_cols], cache[1, :, key_cols]], axis=1)
        values_t = [cache[k, :, value_cols].T for k in range(2)]
        for j in range(2):
            q = heads_t[j]
            none = jnp.zeros_like(q)
            first_q = jnp.where(second_context, 0.0, q)
            second_q = jnp.where(second_context, q, 0.0)
            stack = [first_q, none, second_q, none] if j == 0 else [none, first_q, none, second_q]
            stacked = jnp.concatenate(stack, axis=0).astype(jnp.bfloat16)
            scores = jnp.dot(keys, stacked, preferred_element_type=jnp.float32)
            top = jnp.max(scores, axis=0, keepdims=True)
            weights = jnp.exp(scores - top)
            total = jnp.sum(weights, axis=0, keepdims=True)
            own_rows = slice(j * HEAD_SIZE, (j + 1) * HEAD_SIZE)
            values = jnp.concatenate([v[own_rows] for v in values_t], axis=0)
            out = jnp.dot(
                values, weights.astype(jnp.bfloat16), preferred_element_type=jnp.float32
            )
            out = jnp.where(second_context, out[HEAD_SIZE:], out[:HEAD_SIZE])
            OS[g2, own_rows, :] = out.astype(jnp.bfloat16)
            TS[g2, 2 * j : 2 * j + 1, :] = top
            TS[g2, 2 * j + 1 : 2 * j + 2, :] = total
        for copy in parts_copies(g2):
            copy.start()

    hidden_t[...] = jnp.zeros_like(hidden_t)
    wo_load.wait()

    @pl.loop(0, pairs)
    def _(g2):
        heads_t = transposed_queries(g2)
        key_cols = pl.ds(pl.multiple_of(g2 * pair, 128), pair)
        value_cols = pl.ds(pl.multiple_of(kv_width + g2 * pair, 128), pair)
        own_keys = kv_ref[:, key_cols].astype(jnp.float32).T
        own_values = kv_ref[:, value_cols].astype(jnp.float32).T
        sinks = sink_ref[g2]
        for copy in parts_copies(g2):
            copy.wait()
        mine, theirs = TS[g2], TR[g2]
        stacked = []
        for j in range(2):
            own_rows = slice(j * HEAD_SIZE, (j + 1) * HEAD_SIZE)
            own_key = jnp.concatenate([own_keys[own_rows]] * per, axis=1)
            own_value = jnp.concatenate([own_values[own_rows]] * per, axis=1)
            own_score = jnp.sum(heads_t[j] * own_key, axis=0, keepdims=True)
            sink = sinks[j : j + 1]
            top_a, top_b = mine[2 * j : 2 * j + 1], theirs[2 * j : 2 * j + 1]
            peak = jnp.maximum(jnp.maximum(top_a, top_b), jnp.maximum(own_score, sink))
            factor_a = jnp.exp(top_a - peak)
            factor_b = jnp.exp(top_b - peak)
            own_factor = jnp.exp(own_score - peak)
            denominator = (
                mine[2 * j + 1 : 2 * j + 2] * factor_a
                + theirs[2 * j + 1 : 2 * j + 2] * factor_b
                + own_factor
                + jnp.exp(sink - peak)
            )
            out = (
                OS[g2, own_rows, :].astype(jnp.float32) * factor_a
                + OR[g2, own_rows, :].astype(jnp.float32) * factor_b
                + own_factor * own_value
            ) / denominator
            stacked += [out[:, h * rows : (h + 1) * rows] for h in range(per)]
        attention_t = jnp.concatenate(stacked, axis=0).astype(jnp.bfloat16)
        cols = pl.ds(pl.multiple_of(g2 * 2 * per * HEAD_SIZE, 128), 2 * per * HEAD_SIZE)
        hidden_t[...] += jnp.dot(wo[:, cols], attention_t, preferred_element_type=jnp.float32)

    hidden = hidden_t[...].T + residual_ref[...].astype(jnp.float32)
    attended_ref[...] = hidden.astype(jnp.bfloat16)
    squares = jnp.sum(hidden * hidden, axis=1, keepdims=True)
    squares = jnp.sum(
        jnp.where(eye, jnp.broadcast_to(squares, (rows, rows)), 0.0), axis=0, keepdims=True
    )
    META[a, e] = jnp.concatenate(
        [share_ref[...], jnp.broadcast_to(squares, (experts, rows))], axis=1
    )
    X[a, e] = (hidden * gain_ref[...].astype(jnp.float32)).astype(jnp.bfloat16)

    pending = []
    counter = [0]

    def send(h, idx, target):
        k = counter[0]
        counter[0] += 1
        for ref, sent, received in ((X, xsend, xrecv), (META, msend, mrecv)):
            copy = pltpu.make_async_remote_copy(
                src_ref=ref.at[h, idx],
                dst_ref=ref.at[h, idx],
                send_sem=sent.at[k],
                recv_sem=received.at[h, idx],
                device_id=target,
                device_id_type=MESH,
            )
            copy.start()
            pending.append(copy)

    def arrived(h, idx):
        for ref, sent, received in ((X, xsend, xrecv), (META, msend, mrecv)):
            pltpu.make_async_remote_copy(
                src_ref=ref.at[h, idx],
                dst_ref=ref.at[h, idx],
                send_sem=sent.at[0],
                recv_sem=received.at[h, idx],
                device_id=mate,
                device_id_type=MESH,
            ).wait_recv()

    send(a, e, across)
    for chip in others:
        send(a, e, {"exp": chip * 2 + c})
    send(a, e, mate)

    def pass_on(chip):
        idx = chip * 2 + c
        arrived(a, idx)
        send(a, idx, across)
        send(a, idx, mate)

    def crossed(chip):
        idx = chip * 2 + c
        arrived(1 - a, idx)
        send(1 - a, idx, mate)

    def mates(chip):
        for h in (a, 1 - a):
            arrived(h, chip * 2 + 1 - c)

    def upright(row):
        return jnp.sum(jnp.where(eye, jnp.broadcast_to(row, (rows, rows)), 0.0), axis=1, keepdims=True)

    def run_chunk(chips):
        blocks = [chip * 2 + k for chip in chips for k in range(2)]
        count = len(blocks) * rows
        x = jnp.concatenate(
            [jnp.concatenate([X[0, b], X[1, b]], axis=1) for b in blocks], axis=0
        )
        shares, inverses = [], []
        pick = lax.broadcasted_iota(jnp.int32, (experts, 2 * rows), 0) == e
        for b in blocks:
            squares = META[0, b][0:1, rows : 2 * rows] + META[1, b][0:1, rows : 2 * rows]
            inverses.append(upright(lax.rsqrt(squares / (2 * width) + 1e-05)))
            mine = jnp.sum(jnp.where(pick, META[0, b], 0.0), axis=0, keepdims=True)
            shares.append(upright(mine[:, :rows]))
        inverse = jnp.concatenate(inverses, axis=0)
        share = jnp.concatenate(shares, axis=0)

        def first(start, size):
            cols = pl.ds(start, size)
            g = lax.dot_general(x, wg[cols, :], NT, preferred_element_type=jnp.float32)
            u = lax.dot_general(x, wu[cols, :], NT, preferred_element_type=jnp.float32)
            g = jnp.minimum(g * inverse, clamp_limit)
            u = jnp.clip(u * inverse, -clamp_limit, clamp_limit)
            act_ref[:, cols] = (g * jax.nn.sigmoid(1.702 * g) * (u + 1.0)).astype(jnp.bfloat16)

        def second(start, size):
            cols = pl.ds(start, size)
            y = jnp.dot(act_ref[...], wd[:, cols], preferred_element_type=jnp.float32)
            y = (y * share).astype(jnp.bfloat16)
            for k, b in enumerate(blocks):
                P_ref[b, :, cols] = y[k * rows : (k + 1) * rows]

        return first, second

    def tiled(body, total, tile, start, stop):
        whole_tiles = total // tile

        @pl.loop(start, min(stop, whole_tiles))
        def _(i):
            body(pl.multiple_of(i * tile, tile), tile)

        if total % tile and stop > whole_tiles:
            body(whole_tiles * tile, total % tile)

    tile = 256
    first_tiles = -(-width // tile)
    second_tiles = -(-2 * width // tile)

    def swap(chip, k):
        copy = pltpu.make_async_remote_copy(
            src_ref=P_ref.at[chip * 2 + 1 - c],
            dst_ref=CS.at[chip],
            send_sem=csend.at[k],
            recv_sem=crecv.at[chip],
            device_id=mate,
            device_id_type=MESH,
        )
        copy.start()
        return copy

    def halve(chip, k, swapped):
        swapped.wait()
        total = P_ref[chip * 2 + c].astype(jnp.float32) + CS[chip].astype(jnp.float32)
        low, high = total[:, :width], total[:, width:]
        KEEP[chip] = jnp.where(a == 0, low, high)
        YS[chip] = jnp.where(a == 0, high, low).astype(jnp.bfloat16)
        copy = pltpu.make_async_remote_copy(
            src_ref=YS.at[chip],
            dst_ref=YR.at[chip],
            send_sem=ysend.at[k],
            recv_sem=yrecv.at[chip],
            device_id=across,
            device_id_type=MESH,
        )
        copy.start()
        return copy

    def deliver(chip, k, halved):
        halved.wait()
        ZS[chip] = (KEEP[chip] + YR[chip].astype(jnp.float32)).astype(jnp.bfloat16)
        copy = pltpu.make_async_remote_copy(
            src_ref=ZS.at[chip],
            dst_ref=ZR.at[z],
            send_sem=rsend.at[k],
            recv_sem=rrecv.at[z],
            device_id={"exp": chip * 2 + c},
            device_id_type=MESH,
        )
        copy.start()
        pending.append(copy)

    crossed(z)
    pass_on(groups_of_chips[0][1])
    crossed(groups_of_chips[0][1])
    for chip in groups_of_chips[0]:
        mates(chip)
    loads[0].wait()
    loads[1].wait()
    halved = {}
    position = 0
    swaps = []
    for number, chips in enumerate(groups_of_chips):
        coming = groups_of_chips[number + 1] if number + 1 < pair_count else []
        first, second = run_chunk(chips)
        if coming:
            tiled(first, width, tile, 0, 3)
            pass_on(coming[0])
            tiled(first, width, tile, 3, first_tiles)
            pass_on(coming[1])
        else:
            tiled(first, width, tile, 0, first_tiles)
        for chip, k, swapped in swaps:
            halved[k] = (chip, halve(chip, k, swapped))
        if number == 0:
            loads[2].wait()
        if coming:
            tiled(second, 2 * width, tile, 0, second_tiles // 2)
            crossed(coming[0])
            tiled(second, 2 * width, tile, second_tiles // 2, second_tiles)
            crossed(coming[1])
        else:
            tiled(second, 2 * width, tile, 0, second_tiles)
        swaps = []
        for chip in chips:
            swaps.append((chip, position, swap(chip, position)))
            position += 1
        for k in list(halved):
            if k > 0:
                deliver(halved[k][0], k, halved.pop(k)[1])
        for chip in coming:
            mates(chip)
    for chip, k, swapped in swaps:
        halved[k] = (chip, halve(chip, k, swapped))
    for k in sorted(halved):
        if k > 0:
            deliver(halved[k][0], k, halved[k][1])
    halved[0][1].wait()
    total = KEEP[z] + YR[z].astype(jnp.float32)
    for chip in others:
        pltpu.make_async_remote_copy(
            src_ref=ZR.at[chip],
            dst_ref=ZR.at[chip],
            send_sem=rsend.at[0],
            recv_sem=rrecv.at[chip],
            device_id=mate,
            device_id_type=MESH,
        ).wait_recv()
        total += ZR[chip].astype(jnp.float32)
    out_ref[...] = total.astype(jnp.bfloat16)
    for copy in pending:
        copy.wait_send()


def layer(
    queries, row_key_value, cache, branch, sinks, w_out, residual, gain, by_expert, w_gate, w_up, w_down
):
    n = lax.axis_size("exp")
    rings = n // 2
    rows, width = residual.shape
    per = QUERY_HEADS // KEY_VALUE_HEADS
    pairs = KEY_VALUE_HEADS // 2
    full = 2 * width
    experts = by_expert.shape[0]
    per_chunk = 4 * rows
    sends = 4 * n + 8
    bf = jnp.bfloat16
    dma = pltpu.SemaphoreType.DMA
    return pl.pallas_call(
        functools.partial(layer_kernel, n),
        out_shape=[jax.ShapeDtypeStruct((rows, width), bf)] * 2,
        in_specs=[pl.BlockSpec(memory_space=pltpu.VMEM)] * 7
        + [pl.BlockSpec(memory_space=pl.ANY)] * 5,
        out_specs=[pl.BlockSpec(memory_space=pltpu.VMEM)] * 2,
        scratch_shapes=[
            pltpu.VMEM(cache.shape, bf),
            pltpu.VMEM((width, QUERY_HEADS * HEAD_SIZE), bf),
            pltpu.VMEM((width, rows), jnp.float32),
            pltpu.VMEM((pairs, 2 * HEAD_SIZE, per * rows), bf),
            pltpu.VMEM((pairs, 2 * HEAD_SIZE, per * rows), bf),
            pltpu.VMEM((pairs, 8, per * rows), jnp.float32),
            pltpu.VMEM((pairs, 8, per * rows), jnp.float32),
            dma((pairs,)),
            dma((pairs,)),
            dma((pairs,)),
            dma((pairs,)),
            pltpu.VMEM((width, full), bf),
            pltpu.VMEM((width, full), bf),
            pltpu.VMEM((width, full), bf),
            pltpu.VMEM((2, n, rows, width), bf),
            pltpu.VMEM((2, n, experts, 2 * rows), jnp.float32),
            pltpu.VMEM((per_chunk, width), bf),
            pltpu.VMEM((n, rows, full), bf),
            pltpu.VMEM((rings, rows, full), bf),
            pltpu.VMEM((rings, rows, width), jnp.float32),
            pltpu.VMEM((rings, rows, width), bf),
            pltpu.VMEM((rings, rows, width), bf),
            pltpu.VMEM((rings, rows, width), bf),
            pltpu.VMEM((rings, rows, width), bf),
            dma((5,)),
            dma((sends,)),
            dma((2, n)),
            dma((sends,)),
            dma((2, n)),
            dma((rings,)),
            dma((rings,)),
            dma((rings,)),
            dma((rings,)),
            dma((rings,)),
            dma((rings,)),
        ],
        compiler_params=pltpu.CompilerParams(
            collective_id=1, has_side_effects=True, vmem_limit_bytes=62 * 1024 * 1024
        ),
    )(
        queries,
        row_key_value,
        jnp.tile(branch, per)[None, :],
        jnp.repeat(sinks, rows).reshape(pairs, 2, per * rows),
        residual,
        gain[None, :],
        by_expert,
        cache,
        w_out.T,
        jnp.swapaxes(w_gate, 1, 2),
        jnp.swapaxes(w_up, 1, 2),
        w_down,
    )


def share_table(expert_ids, weight_codes, expert_count):
    shares = weight_codes.astype(jnp.float32)
    shares = shares / jnp.sum(shares, axis=1, keepdims=True)
    named = expert_ids[None, :, :] == jnp.arange(expert_count, dtype=jnp.int32)[:, None, None]
    return jnp.sum(jnp.where(named, shares[None], 0.0), axis=2)


def routed_experts(hidden, norm_gain, expert_ids, weight_codes, w_gate, w_up, w_down):
    decode_row_count = hidden.shape[0]
    squares = lax.psum(jnp.sum(hidden * hidden, axis=1), "att")
    inverse = lax.rsqrt(squares / D + 1e-05)
    normed = (hidden * inverse[:, None] * norm_gain.astype(jnp.float32)[None, :]).astype(
        jnp.bfloat16
    )
    local_experts = w_gate.shape[0]
    expert_count = local_experts * lax.axis_size("exp")
    capacity = min(decode_row_count, max(2, 2 * decode_row_count * TOP // expert_count))
    flat_ids = expert_ids.reshape(-1)
    expert_hits = (flat_ids[:, None] == jnp.arange(expert_count, dtype=jnp.int32)[None, :]).astype(
        jnp.int32
    )
    earlier = jnp.cumsum(expert_hits, axis=0) - expert_hits
    position = jnp.sum(earlier * expert_hits, axis=1)
    slot_index = flat_ids * capacity + position
    placed = slot_index[None, :] == jnp.arange(expert_count * capacity, dtype=jnp.int32)[:, None]
    assign = jnp.any(placed.reshape(expert_count * capacity, decode_row_count, TOP), axis=2).astype(
        jnp.bfloat16
    )
    source_rows = lax.all_gather(normed, "att", axis=1, tiled=True)
    outgoing = jnp.dot(assign, source_rows, preferred_element_type=jnp.float32).astype(jnp.bfloat16)
    outgoing = outgoing.reshape(expert_count, capacity, -1)
    received = lax.all_to_all(outgoing, "exp", split_axis=0, concat_axis=0, tiled=True)
    senders = received.shape[0] // local_experts
    slot_count = received.shape[1]
    arranged = received.reshape(senders, local_experts, slot_count, received.shape[2])
    gate_sum = jnp.einsum("sekd,edf->sekf", arranged, w_gate, preferred_element_type=jnp.float32)
    up_sum = jnp.einsum("sekd,edf->sekf", arranged, w_up, preferred_element_type=jnp.float32)
    gate_sum = jnp.minimum(gate_sum, clamp_limit)
    up_sum = jnp.clip(up_sum, -clamp_limit, clamp_limit)
    active = (gate_sum * jax.nn.sigmoid(1.702 * gate_sum) * (up_sum + 1.0)).astype(jnp.bfloat16)
    partial_out = jnp.einsum("sekf,efd->sekd", active, w_down, preferred_element_type=jnp.float32)
    summed = lax.psum_scatter(
        partial_out.astype(jnp.bfloat16), "att", scatter_dimension=3, tiled=True
    )
    answer = lax.all_to_all(
        summed.reshape(senders * local_experts, slot_count, -1),
        "exp",
        split_axis=0,
        concat_axis=0,
        tiled=True,
    )
    flat_returned = answer.reshape(expert_count * capacity, -1)
    picked = flat_returned[slot_index].reshape(decode_row_count, TOP, -1).astype(jnp.float32)
    shares = weight_codes.astype(jnp.float32)
    shares = shares / jnp.sum(shares, axis=1, keepdims=True)
    mixture = jnp.sum(picked * shares[:, :, None], axis=1).astype(jnp.bfloat16)
    return mixture


def shards(
    queries,
    row_key_value,
    shared_context_cache,
    branch,
    sink_logits,
    w_out,
    residual,
    norm_gain,
    expert_ids,
    weight_codes,
    w_gate,
    w_up,
    w_down,
):
    near = lax.axis_size("att") == 2 and lax.axis_size("exp") % 4 == 0 and w_gate.shape[0] == 1
    if near:
        return layer(
            queries,
            row_key_value,
            shared_context_cache,
            branch,
            sink_logits,
            w_out,
            residual,
            norm_gain,
            share_table(expert_ids, weight_codes, w_gate.shape[0] * lax.axis_size("exp")),
            w_gate,
            w_up,
            w_down,
        )
    decode_row_count = queries.shape[0]
    grouped_heads = queries.reshape(
        decode_row_count, KEY_VALUE_HEADS, QUERY_HEADS // KEY_VALUE_HEADS, HEAD_SIZE
    )
    partial_stats = local_partials(grouped_heads, shared_context_cache, branch)
    merged = combined_all(partial_stats, "att", merge_parts)
    attention = finish_attention(merged, grouped_heads, row_key_value, sink_logits)
    projected = jnp.dot(attention, w_out, preferred_element_type=jnp.float32)
    hidden = residual.astype(jnp.float32) + projected
    attended = hidden.astype(jnp.bfloat16)
    mixture = routed_experts(
        hidden, norm_gain, expert_ids, weight_codes, w_gate, w_up, w_down
    )
    return (attended, mixture)


def solution(mesh):
    placed = (
        P(("groups", "exp"), None),
        P(("groups", "exp"), None),
        P("groups", "att", None),
        P(("groups", "exp")),
        P(),
        P(None, "att"),
        P(("groups", "exp"), "att"),
        P("att"),
        P(("groups", "exp"), None),
        P(("groups", "exp"), None),
        P("exp", None, "att"),
        P("exp", None, "att"),
        P("exp", "att", None),
    )
    return jax.shard_map(
        shards,
        mesh=mesh,
        in_specs=placed,
        out_specs=(P(("groups", "exp"), "att"), P(("groups", "exp"), "att")),
        check_vma=False,
    )
```

```python
import functools

import jax
import jax.numpy as jnp
from jax import lax
from jax.experimental import pallas as pl
from jax.experimental.pallas import tpu as pltpu
from jax.sharding import PartitionSpec as P

D = 2880
QUERY_HEADS = 64
KEY_VALUE_HEADS = 8
HEAD_SIZE = 64
TOP = 4
SHARED_CONTEXTS = 2


MESH = pl.DeviceIdType.MESH
NT = (((1,), (1,)), ((), ()))
clamp_limit = 7.0


def combined_all(x, axis, combine):
    everything = jax.tree.map(
        lambda part, kind: lax.all_gather(part.astype(kind), axis),
        x,
        jax.tree.map(lambda a: jnp.bfloat16 if a.dtype == jnp.float32 else a.dtype, x),
    )

    def take(k):
        return jax.tree.map(lambda part, own: part[k].astype(own.dtype), everything, x)

    return lax.fori_loop(
        1, lax.axis_size(axis), lambda k, so_far: combine(so_far, take(k)), take(0)
    )


def merge_parts(first, second):
    first_max, first_total, first_out = first
    second_max, second_total, second_out = second
    joint_max = jnp.maximum(first_max, second_max)
    first_factor = jnp.exp(first_max - joint_max)
    second_factor = jnp.exp(second_max - joint_max)
    joint_total = first_total * first_factor + second_total * second_factor
    decode_row_count, head_count = first_max.shape
    joint_out = (
        first_out.reshape(decode_row_count, head_count, -1) * first_factor[:, :, None]
        + second_out.reshape(decode_row_count, head_count, -1) * second_factor[:, :, None]
    )
    return (joint_max, joint_total, joint_out.reshape(decode_row_count, -1))


def local_partials(grouped_heads, shared_context_cache, branch):
    decode_row_count = grouped_heads.shape[0]
    score_scale = HEAD_SIZE ** (-0.5)
    current = None
    for context_slot in range(SHARED_CONTEXTS):
        cached_key_block = shared_context_cache[
            context_slot, :, : KEY_VALUE_HEADS * HEAD_SIZE
        ].reshape(-1, KEY_VALUE_HEADS, HEAD_SIZE)
        cached_value_block = shared_context_cache[
            context_slot, :, KEY_VALUE_HEADS * HEAD_SIZE :
        ].reshape(-1, KEY_VALUE_HEADS, HEAD_SIZE)
        scores = (
            jnp.einsum(
                "rgqd,tgd->rgqt",
                grouped_heads,
                cached_key_block,
                preferred_element_type=jnp.float32,
            )
            * score_scale
        )
        local_max = jnp.max(scores, axis=-1)
        weights = jnp.exp(scores - local_max[..., None])
        local_total = jnp.sum(weights, axis=-1)
        local_out = jnp.einsum(
            "rgqt,tgd->rgqd",
            weights.astype(jnp.bfloat16),
            cached_value_block,
            preferred_element_type=jnp.float32,
        )
        if current is None:
            current = (local_max, local_total, local_out)
        else:
            chosen = branch == context_slot
            current = (
                jnp.where(chosen[:, None, None], local_max, current[0]),
                jnp.where(chosen[:, None, None], local_total, current[1]),
                jnp.where(chosen[:, None, None, None], local_out, current[2]),
            )
    return (
        current[0].reshape(decode_row_count, QUERY_HEADS),
        current[1].reshape(decode_row_count, QUERY_HEADS),
        current[2].reshape(decode_row_count, QUERY_HEADS * HEAD_SIZE),
    )


def finish_attention(merged, grouped_heads, row_key_value, sink_logits):
    decode_row_count = grouped_heads.shape[0]
    heads_per_group = QUERY_HEADS // KEY_VALUE_HEADS
    score_scale = HEAD_SIZE ** (-0.5)
    cache_max, cache_total, cache_out = merged
    row_own_keys = (
        row_key_value[:, : KEY_VALUE_HEADS * HEAD_SIZE]
        .reshape(decode_row_count, KEY_VALUE_HEADS, 1, HEAD_SIZE)
        .astype(jnp.float32)
    )
    row_own_values = (
        row_key_value[:, KEY_VALUE_HEADS * HEAD_SIZE :]
        .reshape(decode_row_count, KEY_VALUE_HEADS, 1, HEAD_SIZE)
        .astype(jnp.float32)
    )
    own_score = (
        jnp.sum(grouped_heads.astype(jnp.float32) * row_own_keys, axis=-1) * score_scale
    ).reshape(decode_row_count, QUERY_HEADS)
    row_own_values = jnp.broadcast_to(
        row_own_values, (decode_row_count, KEY_VALUE_HEADS, heads_per_group, HEAD_SIZE)
    ).reshape(decode_row_count, QUERY_HEADS, HEAD_SIZE)
    sink_row = sink_logits[None, :]
    peak = jnp.maximum(jnp.maximum(cache_max, own_score), sink_row)
    cache_factor = jnp.exp(cache_max - peak)
    own_factor = jnp.exp(own_score - peak)
    sink_factor = jnp.exp(sink_row - peak)
    denominator = cache_total * cache_factor + own_factor + sink_factor
    numerator = (
        cache_out.reshape(decode_row_count, QUERY_HEADS, HEAD_SIZE) * cache_factor[..., None]
        + own_factor[..., None] * row_own_values
    )
    return (
        (numerator / denominator[..., None])
        .reshape(decode_row_count, QUERY_HEADS * HEAD_SIZE)
        .astype(jnp.bfloat16)
    )

def layer_kernel(
    n,
    q_ref,
    kv_ref,
    branch_ref,
    sink_ref,
    residual_ref,
    gain_ref,
    ids_ref,
    codes_ref,
    cache_hbm,
    wo_hbm,
    wg_hbm,
    wu_hbm,
    wd_hbm,
    attended_ref,
    out_ref,
    cache,
    wo,
    hidden_t,
    OS,
    OR,
    TS,
    TR,
    osend,
    orecv,
    tsend,
    trecv,
    wg,
    wu,
    wd,
    X,
    META,
    act_ref,
    P_ref,
    CS,
    KEEP,
    ZS,
    ZR,
    YS,
    YR,
    wsem,
    xsend,
    xrecv,
    msend,
    mrecv,
    csend,
    crecv,
    rsend,
    rrecv,
    ysend,
    yrecv,
):
    rings = n // 2
    rows = residual_ref.shape[0]
    width = residual_ref.shape[1]
    experts = META.shape[2]
    a = lax.axis_index("att")
    e = lax.axis_index("exp")
    z = e // 2
    c = e % 2

    pair_count = rings // 2
    side = z % 2
    groups_of_chips = []
    for k in range(pair_count):
        base = lax.rem(z // 2 + k, pair_count) * 2
        groups_of_chips.append([base + side, base + 1 - side] if k == 0 else [base + 1 - side, base + side])
    others = [chip for group in groups_of_chips for chip in group][1:]
    mate = {"exp": z * 2 + 1 - c}
    across = {"att": 1 - a}

    cache_load = pltpu.make_async_copy(cache_hbm, cache, wsem.at[3])
    cache_load.start()
    wo_load = pltpu.make_async_copy(wo_hbm, wo, wsem.at[4])
    wo_load.start()
    loads = [
        pltpu.make_async_copy(wg_hbm.at[0], wg, wsem.at[0]),
        pltpu.make_async_copy(wu_hbm.at[0], wu, wsem.at[1]),
        pltpu.make_async_copy(wd_hbm.at[0], wd, wsem.at[2]),
    ]
    for load in loads:
        load.start()

    barrier = pltpu.get_barrier_semaphore()
    for target in [mate, across] + [{"exp": chip * 2 + c} for chip in others]:
        pl.semaphore_signal(barrier, inc=1, device_id=target, device_id_type=MESH)
    pl.semaphore_wait(barrier, rings + 1)
    eye = lax.broadcasted_iota(jnp.int32, (rows, rows), 0) == lax.broadcasted_iota(
        jnp.int32, (rows, rows), 1
    )

    per = QUERY_HEADS // KEY_VALUE_HEADS
    columns = per * rows
    pair = 2 * HEAD_SIZE
    pairs = KEY_VALUE_HEADS // 2
    kv_width = KEY_VALUE_HEADS * HEAD_SIZE
    second_context = jnp.concatenate([branch_ref[...]] * per, axis=1) == 1

    def transposed_queries(g2):
        start = pl.multiple_of(g2 * 2 * per * HEAD_SIZE, 128)
        block = q_ref[:, pl.ds(start, 2 * per * HEAD_SIZE)].astype(jnp.float32).T
        block = block * HEAD_SIZE ** (-0.5)

        def head(k):
            return block[k * HEAD_SIZE : (k + 1) * HEAD_SIZE]

        return [
            jnp.concatenate([head(j * per + h) for h in range(per)], axis=1) for j in range(2)
        ]

    def parts_copies(g2):
        return (
            pltpu.make_async_remote_copy(
                src_ref=OS.at[g2],
                dst_ref=OR.at[g2],
                send_sem=osend.at[g2],
                recv_sem=orecv.at[g2],
                device_id=across,
                device_id_type=MESH,
            ),
            pltpu.make_async_remote_copy(
                src_ref=TS.at[g2],
                dst_ref=TR.at[g2],
                send_sem=tsend.at[g2],
                recv_sem=trecv.at[g2],
                device_id=across,
                device_id_type=MESH,
            ),
        )

    cache_load.wait()

    @pl.loop(0, pairs)
    def _(g2):
        heads_t = transposed_queries(g2)
        key_cols = pl.ds(pl.multiple_of(g2 * pair, 128), pair)
        value_cols = pl.ds(pl.multiple_of(kv_width + g2 * pair, 128), pair)
        keys = jnp.concatenate([cache[0, :, key_cols], cache[1, :, key_cols]], axis=1)
        values_t = [cache[k, :, value_cols].T for k in range(2)]
        for j in range(2):
            q = heads_t[j]
            none = jnp.zeros_like(q)
            first_q = jnp.where(second_context, 0.0, q)
            second_q = jnp.where(second_context, q, 0.0)
            stack = [first_q, none, second_q, none] if j == 0 else [none, first_q, none, second_q]
            stacked = jnp.concatenate(stack, axis=0).astype(jnp.bfloat16)
            scores = jnp.dot(keys, stacked, preferred_element_type=jnp.float32)
            top = jnp.max(scores, axis=0, keepdims=True)
            weights = jnp.exp(scores - top)
            total = jnp.sum(weights, axis=0, keepdims=True)
            own_rows = slice(j * HEAD_SIZE, (j + 1) * HEAD_SIZE)
            values = jnp.concatenate([v[own_rows] for v in values_t], axis=0)
            out = jnp.dot(
                values, weights.astype(jnp.bfloat16), preferred_element_type=jnp.float32
            )
            out = jnp.where(second_context, out[HEAD_SIZE:], out[:HEAD_SIZE])
            OS[g2, own_rows, :] = out.astype(jnp.bfloat16)
            TS[g2, 2 * j : 2 * j + 1, :] = top
            TS[g2, 2 * j + 1 : 2 * j + 2, :] = total
        for copy in parts_copies(g2):
            copy.start()

    hidden_t[...] = jnp.zeros_like(hidden_t)
    wo_load.wait()

    @pl.loop(0, pairs)
    def _(g2):
        heads_t = transposed_queries(g2)
        key_cols = pl.ds(pl.multiple_of(g2 * pair, 128), pair)
        value_cols = pl.ds(pl.multiple_of(kv_width + g2 * pair, 128), pair)
        own_keys = kv_ref[:, key_cols].astype(jnp.float32).T
        own_values = kv_ref[:, value_cols].astype(jnp.float32).T
        for copy in parts_copies(g2):
            copy.wait()
        mine, theirs = TS[g2], TR[g2]
        stacked = []
        for j in range(2):
            own_rows = slice(j * HEAD_SIZE, (j + 1) * HEAD_SIZE)
            own_key = jnp.concatenate([own_keys[own_rows]] * per, axis=1)
            own_value = jnp.concatenate([own_values[own_rows]] * per, axis=1)
            own_score = jnp.sum(heads_t[j] * own_key, axis=0, keepdims=True)
            sink = jnp.concatenate(
                [jnp.full((1, rows), sink_ref[(g2 * 2 + j) * per + h]) for h in range(per)], axis=1
            )
            top_a, top_b = mine[2 * j : 2 * j + 1], theirs[2 * j : 2 * j + 1]
            peak = jnp.maximum(jnp.maximum(top_a, top_b), jnp.maximum(own_score, sink))
            factor_a = jnp.exp(top_a - peak)
            factor_b = jnp.exp(top_b - peak)
            own_factor = jnp.exp(own_score - peak)
            denominator = (
                mine[2 * j + 1 : 2 * j + 2] * factor_a
                + theirs[2 * j + 1 : 2 * j + 2] * factor_b
                + own_factor
                + jnp.exp(sink - peak)
            )
            out = (
                OS[g2, own_rows, :].astype(jnp.float32) * factor_a
                + OR[g2, own_rows, :].astype(jnp.float32) * factor_b
                + own_factor * own_value
            ) / denominator
            stacked += [out[:, h * rows : (h + 1) * rows] for h in range(per)]
        attention_t = jnp.concatenate(stacked, axis=0).astype(jnp.bfloat16)
        cols = pl.ds(pl.multiple_of(g2 * 2 * per * HEAD_SIZE, 128), 2 * per * HEAD_SIZE)
        hidden_t[...] += jnp.dot(wo[:, cols], attention_t, preferred_element_type=jnp.float32)

    hidden = hidden_t[...].T + residual_ref[...].astype(jnp.float32)
    attended_ref[...] = hidden.astype(jnp.bfloat16)
    squares = jnp.sum(hidden * hidden, axis=1, keepdims=True)
    squares = jnp.sum(
        jnp.where(eye, jnp.broadcast_to(squares, (rows, rows)), 0.0), axis=0, keepdims=True
    )
    codes = codes_ref[...].astype(jnp.float32)
    codes = codes / jnp.sum(codes, axis=0, keepdims=True)
    row_of = lax.broadcasted_iota(jnp.int32, (experts, rows), 0)
    table = jnp.zeros((experts, rows), jnp.float32)
    for k in range(TOP):
        table += jnp.where(row_of == ids_ref[k : k + 1, :], codes[k : k + 1, :], 0.0)
    META[a, e] = jnp.concatenate(
        [table, jnp.broadcast_to(squares, (experts, rows))], axis=1
    )
    X[a, e] = (hidden * gain_ref[...].astype(jnp.float32)).astype(jnp.bfloat16)

    pending = []
    counter = [0]

    def send(h, idx, target):
        k = counter[0]
        counter[0] += 1
        for ref, sent, received in ((X, xsend, xrecv), (META, msend, mrecv)):
            copy = pltpu.make_async_remote_copy(
                src_ref=ref.at[h, idx],
                dst_ref=ref.at[h, idx],
                send_sem=sent.at[k],
                recv_sem=received.at[h, idx],
                device_id=target,
                device_id_type=MESH,
            )
            copy.start()
            pending.append(copy)

    def arrived(h, idx):
        for ref, sent, received in ((X, xsend, xrecv), (META, msend, mrecv)):
            pltpu.make_async_remote_copy(
                src_ref=ref.at[h, idx],
                dst_ref=ref.at[h, idx],
                send_sem=sent.at[0],
                recv_sem=received.at[h, idx],
                device_id=mate,
                device_id_type=MESH,
            ).wait_recv()

    send(a, e, across)
    twin, far, farther = others
    for chip in (twin, far):
        send(a, e, {"exp": chip * 2 + c})
    send(a, e, mate)

    def pass_on(chip):
        idx = chip * 2 + c
        arrived(a, idx)
        send(a, idx, across)
        if chip is far:
            send(a, idx, {"exp": twin * 2 + c})
        send(a, idx, mate)

    def crossed(chip):
        idx = chip * 2 + c
        arrived(1 - a, idx)
        send(1 - a, idx, mate)

    def mates(chip):
        for h in (a, 1 - a):
            arrived(h, chip * 2 + 1 - c)

    def upright(row):
        return jnp.sum(jnp.where(eye, jnp.broadcast_to(row, (rows, rows)), 0.0), axis=1, keepdims=True)

    def run_chunk(chips):
        blocks = [chip * 2 + k for chip in chips for k in range(2)]
        count = len(blocks) * rows
        x = jnp.concatenate(
            [jnp.concatenate([X[0, b], X[1, b]], axis=1) for b in blocks], axis=0
        )
        shares, inverses = [], []
        pick = lax.broadcasted_iota(jnp.int32, (experts, 2 * rows), 0) == e
        for b in blocks:
            squares = META[0, b][0:1, rows : 2 * rows] + META[1, b][0:1, rows : 2 * rows]
            inverses.append(upright(lax.rsqrt(squares / (2 * width) + 1e-05)))
            mine = jnp.sum(jnp.where(pick, META[0, b], 0.0), axis=0, keepdims=True)
            shares.append(upright(mine[:, :rows]))
        inverse = jnp.concatenate(inverses, axis=0)
        share = jnp.concatenate(shares, axis=0)

        def first(start, size):
            cols = pl.ds(start, size)
            g = lax.dot_general(x, wg[cols, :], NT, preferred_element_type=jnp.float32)
            u = lax.dot_general(x, wu[cols, :], NT, preferred_element_type=jnp.float32)
            g = jnp.minimum(g * inverse, clamp_limit)
            u = jnp.clip(u * inverse, -clamp_limit, clamp_limit)
            act_ref[:, cols] = (g * jax.nn.sigmoid(1.702 * g) * (u + 1.0)).astype(jnp.bfloat16)

        def second(start, size):
            cols = pl.ds(start, size)
            y = jnp.dot(act_ref[...], wd[:, cols], preferred_element_type=jnp.float32)
            y = (y * share).astype(jnp.bfloat16)
            for k, b in enumerate(blocks):
                P_ref[b, :, cols] = y[k * rows : (k + 1) * rows]

        return first, second

    def tiled(body, total, tile, start, stop):
        whole_tiles = total // tile

        @pl.loop(start, min(stop, whole_tiles))
        def _(i):
            body(pl.multiple_of(i * tile, tile), tile)

        if total % tile and stop > whole_tiles:
            body(whole_tiles * tile, total % tile)

    tile = 256
    first_tiles = -(-width // tile)
    second_tiles = -(-2 * width // tile)

    def swap(chip, k):
        copy = pltpu.make_async_remote_copy(
            src_ref=P_ref.at[chip * 2 + 1 - c],
            dst_ref=CS.at[chip],
            send_sem=csend.at[k],
            recv_sem=crecv.at[chip],
            device_id=mate,
            device_id_type=MESH,
        )
        copy.start()
        return copy

    def halve(chip, k, swapped):
        swapped.wait()
        total = P_ref[chip * 2 + c].astype(jnp.float32) + CS[chip].astype(jnp.float32)
        low, high = total[:, :width], total[:, width:]
        KEEP[chip] = jnp.where(a == 0, low, high)
        YS[chip] = jnp.where(a == 0, high, low).astype(jnp.bfloat16)
        copy = pltpu.make_async_remote_copy(
            src_ref=YS.at[chip],
            dst_ref=YR.at[chip],
            send_sem=ysend.at[k],
            recv_sem=yrecv.at[chip],
            device_id=across,
            device_id_type=MESH,
        )
        copy.start()
        return copy

    def landed(slot):
        pltpu.make_async_remote_copy(
            src_ref=ZR.at[slot],
            dst_ref=ZR.at[slot],
            send_sem=rsend.at[0],
            recv_sem=rrecv.at[slot],
            device_id=mate,
            device_id_type=MESH,
        ).wait_recv()
        return ZR[slot].astype(jnp.float32)

    def deliver(chip, k, halved, target, slot):
        halved.wait()
        total = KEEP[chip] + YR[chip].astype(jnp.float32)
        if chip is far:
            total += landed(farther)
        ZS[chip] = total.astype(jnp.bfloat16)
        copy = pltpu.make_async_remote_copy(
            src_ref=ZS.at[chip],
            dst_ref=ZR.at[slot],
            send_sem=rsend.at[k],
            recv_sem=rrecv.at[slot],
            device_id={"exp": target * 2 + c},
            device_id_type=MESH,
        )
        copy.start()
        pending.append(copy)

    crossed(z)
    pass_on(groups_of_chips[0][1])
    crossed(groups_of_chips[0][1])
    for chip in groups_of_chips[0]:
        mates(chip)
    loads[0].wait()
    loads[1].wait()
    halved = {}
    position = 0
    swaps = []
    for number, chips in enumerate(groups_of_chips):
        coming = groups_of_chips[number + 1] if number + 1 < pair_count else []
        first, second = run_chunk(chips)
        if coming:
            tiled(first, width, tile, 0, 3)
            pass_on(coming[0])
            tiled(first, width, tile, 3, first_tiles)
            pass_on(coming[1])
        else:
            tiled(first, width, tile, 0, first_tiles)
        for chip, k, swapped in swaps:
            halved[k] = (chip, halve(chip, k, swapped))
        if number == 0:
            loads[2].wait()
        if coming:
            tiled(second, 2 * width, tile, 0, second_tiles // 2)
            crossed(coming[0])
            tiled(second, 2 * width, tile, second_tiles // 2, second_tiles)
            crossed(coming[1])
        else:
            tiled(second, 2 * width, tile, 0, second_tiles)
        swaps = []
        for chip in chips if number == 0 else chips[::-1]:
            swaps.append((chip, position, swap(chip, position)))
            position += 1
        if 1 in halved:
            deliver(twin, 1, halved[1][1], twin, z)
        for chip in coming:
            mates(chip)
    for chip, k, swapped in swaps:
        halved[k] = (chip, halve(chip, k, swapped))
    deliver(farther, 2, halved[2][1], twin, far)
    deliver(far, 3, halved[3][1], far, z)
    halved[0][1].wait()
    total = KEEP[z] + YR[z].astype(jnp.float32) + landed(twin) + landed(far)
    out_ref[...] = total.astype(jnp.bfloat16)
    for copy in pending:
        copy.wait_send()


def layer(
    queries, row_key_value, cache, branch, sinks, w_out, residual, gain, expert_ids, weight_codes, w_gate, w_up, w_down
):
    n = lax.axis_size("exp")
    rings = n // 2
    rows, width = residual.shape
    per = QUERY_HEADS // KEY_VALUE_HEADS
    pairs = KEY_VALUE_HEADS // 2
    full = 2 * width
    experts = w_gate.shape[0] * n
    per_chunk = 4 * rows
    sends = 4 * n + 8
    bf = jnp.bfloat16
    dma = pltpu.SemaphoreType.DMA
    return pl.pallas_call(
        functools.partial(layer_kernel, n),
        out_shape=[jax.ShapeDtypeStruct((rows, width), bf)] * 2,
        in_specs=[pl.BlockSpec(memory_space=pltpu.VMEM)] * 3
        + [pl.BlockSpec(memory_space=pltpu.SMEM)]
        + [pl.BlockSpec(memory_space=pltpu.VMEM)] * 4
        + [pl.BlockSpec(memory_space=pl.ANY)] * 5,
        out_specs=[pl.BlockSpec(memory_space=pltpu.VMEM)] * 2,
        scratch_shapes=[
            pltpu.VMEM(cache.shape, bf),
            pltpu.VMEM((width, QUERY_HEADS * HEAD_SIZE), bf),
            pltpu.VMEM((width, rows), jnp.float32),
            pltpu.VMEM((pairs, 2 * HEAD_SIZE, per * rows), bf),
            pltpu.VMEM((pairs, 2 * HEAD_SIZE, per * rows), bf),
            pltpu.VMEM((pairs, 8, per * rows), jnp.float32),
            pltpu.VMEM((pairs, 8, per * rows), jnp.float32),
            dma((pairs,)),
            dma((pairs,)),
            dma((pairs,)),
            dma((pairs,)),
            pltpu.VMEM((width, full), bf),
            pltpu.VMEM((width, full), bf),
            pltpu.VMEM((width, full), bf),
            pltpu.VMEM((2, n, rows, width), bf),
            pltpu.VMEM((2, n, experts, 2 * rows), jnp.float32),
            pltpu.VMEM((per_chunk, width), bf),
            pltpu.VMEM((n, rows, full), bf),
            pltpu.VMEM((rings, rows, full), bf),
            pltpu.VMEM((rings, rows, width), jnp.float32),
            pltpu.VMEM((rings, rows, width), bf),
            pltpu.VMEM((rings, rows, width), bf),
            pltpu.VMEM((rings, rows, width), bf),
            pltpu.VMEM((rings, rows, width), bf),
            dma((5,)),
            dma((sends,)),
            dma((2, n)),
            dma((sends,)),
            dma((2, n)),
            dma((rings,)),
            dma((rings,)),
            dma((rings,)),
            dma((rings,)),
            dma((rings,)),
            dma((rings,)),
        ],
        compiler_params=pltpu.CompilerParams(
            collective_id=1, has_side_effects=True, vmem_limit_bytes=62 * 1024 * 1024
        ),
    )(
        queries,
        row_key_value,
        branch[None, :],
        sinks,
        residual,
        gain[None, :],
        expert_ids.T,
        weight_codes.T,
        cache,
        w_out.T,
        jnp.swapaxes(w_gate, 1, 2),
        jnp.swapaxes(w_up, 1, 2),
        w_down,
    )


def routed_experts(hidden, norm_gain, expert_ids, weight_codes, w_gate, w_up, w_down):
    decode_row_count = hidden.shape[0]
    squares = lax.psum(jnp.sum(hidden * hidden, axis=1), "att")
    inverse = lax.rsqrt(squares / D + 1e-05)
    normed = (hidden * inverse[:, None] * norm_gain.astype(jnp.float32)[None, :]).astype(
        jnp.bfloat16
    )
    local_experts = w_gate.shape[0]
    expert_count = local_experts * lax.axis_size("exp")
    capacity = min(decode_row_count, max(2, 2 * decode_row_count * TOP // expert_count))
    flat_ids = expert_ids.reshape(-1)
    expert_hits = (flat_ids[:, None] == jnp.arange(expert_count, dtype=jnp.int32)[None, :]).astype(
        jnp.int32
    )
    earlier = jnp.cumsum(expert_hits, axis=0) - expert_hits
    position = jnp.sum(earlier * expert_hits, axis=1)
    slot_index = flat_ids * capacity + position
    placed = slot_index[None, :] == jnp.arange(expert_count * capacity, dtype=jnp.int32)[:, None]
    assign = jnp.any(placed.reshape(expert_count * capacity, decode_row_count, TOP), axis=2).astype(
        jnp.bfloat16
    )
    source_rows = lax.all_gather(normed, "att", axis=1, tiled=True)
    outgoing = jnp.dot(assign, source_rows, preferred_element_type=jnp.float32).astype(jnp.bfloat16)
    outgoing = outgoing.reshape(expert_count, capacity, -1)
    received = lax.all_to_all(outgoing, "exp", split_axis=0, concat_axis=0, tiled=True)
    senders = received.shape[0] // local_experts
    slot_count = received.shape[1]
    arranged = received.reshape(senders, local_experts, slot_count, received.shape[2])
    gate_sum = jnp.einsum("sekd,edf->sekf", arranged, w_gate, preferred_element_type=jnp.float32)
    up_sum = jnp.einsum("sekd,edf->sekf", arranged, w_up, preferred_element_type=jnp.float32)
    gate_sum = jnp.minimum(gate_sum, clamp_limit)
    up_sum = jnp.clip(up_sum, -clamp_limit, clamp_limit)
    active = (gate_sum * jax.nn.sigmoid(1.702 * gate_sum) * (up_sum + 1.0)).astype(jnp.bfloat16)
    partial_out = jnp.einsum("sekf,efd->sekd", active, w_down, preferred_element_type=jnp.float32)
    summed = lax.psum_scatter(
        partial_out.astype(jnp.bfloat16), "att", scatter_dimension=3, tiled=True
    )
    answer = lax.all_to_all(
        summed.reshape(senders * local_experts, slot_count, -1),
        "exp",
        split_axis=0,
        concat_axis=0,
        tiled=True,
    )
    flat_returned = answer.reshape(expert_count * capacity, -1)
    picked = flat_returned[slot_index].reshape(decode_row_count, TOP, -1).astype(jnp.float32)
    shares = weight_codes.astype(jnp.float32)
    shares = shares / jnp.sum(shares, axis=1, keepdims=True)
    mixture = jnp.sum(picked * shares[:, :, None], axis=1).astype(jnp.bfloat16)
    return mixture


def shards(
    queries,
    row_key_value,
    shared_context_cache,
    branch,
    sink_logits,
    w_out,
    residual,
    norm_gain,
    expert_ids,
    weight_codes,
    w_gate,
    w_up,
    w_down,
):
    near = lax.axis_size("att") == 2 and lax.axis_size("exp") == 8 and w_gate.shape[0] == 1
    if near:
        return layer(
            queries,
            row_key_value,
            shared_context_cache,
            branch,
            sink_logits,
            w_out,
            residual,
            norm_gain,
            expert_ids,
            weight_codes,
            w_gate,
            w_up,
            w_down,
        )
    decode_row_count = queries.shape[0]
    grouped_heads = queries.reshape(
        decode_row_count, KEY_VALUE_HEADS, QUERY_HEADS // KEY_VALUE_HEADS, HEAD_SIZE
    )
    partial_stats = local_partials(grouped_heads, shared_context_cache, branch)
    merged = combined_all(partial_stats, "att", merge_parts)
    attention = finish_attention(merged, grouped_heads, row_key_value, sink_logits)
    projected = jnp.dot(attention, w_out, preferred_element_type=jnp.float32)
    hidden = residual.astype(jnp.float32) + projected
    attended = hidden.astype(jnp.bfloat16)
    mixture = routed_experts(
        hidden, norm_gain, expert_ids, weight_codes, w_gate, w_up, w_down
    )
    return (attended, mixture)


def solution(mesh):
    placed = (
        P(("groups", "exp"), None),
        P(("groups", "exp"), None),
        P("groups", "att", None),
        P(("groups", "exp")),
        P(),
        P(None, "att"),
        P(("groups", "exp"), "att"),
        P("att"),
        P(("groups", "exp"), None),
        P(("groups", "exp"), None),
        P("exp", None, "att"),
        P("exp", None, "att"),
        P("exp", "att", None),
    )
    return jax.shard_map(
        shards,
        mesh=mesh,
        in_specs=placed,
        out_specs=(P(("groups", "exp"), "att"), P(("groups", "exp"), "att")),
        check_vma=False,
    )
```
